512 devices in a mesh: frm: 32 (over z, core), col: 16 (over x, y).
Axes of the slice: x: 4, y: 4, z: 16, core: 2. Of those that a mesh axis runs over, the one named last changes fastest.
Arguments:
- video: bfloat16 [64, 32, 512, 512], P('frm', None, 'col'), may hold values from -6 to 6
- norm_gain: float32 [512], replicated, may hold values from 0.25 to 1.75
- w_query: bfloat16 [512, 512], replicated, may hold values from -1 to 1
- w_key: bfloat16 [512, 512], replicated, may hold values from -1 to 1
- w_value: bfloat16 [512, 512], replicated, may hold values from -0.25 to 0.25
- w_out: bfloat16 [512, 512], replicated, may hold values from -0.25 to 0.25
- w_time: bfloat16 [3, 512, 512], replicated, may hold values from -0.15625 to 0.15625
- w_depth: float32 [3, 3, 512], replicated, may hold values from -2 to 2
Outputs:
- encoded: bfloat16 [32, 32, 512, 512], P('frm', None, 'col')
The draws below stay inside these ranges and needn't reach their ends.
All inputs are finite; a program needn't handle non-finite values.
Results may differ from the reference program's by a relative error of at most 0.012.
The reference program's roundings to bfloat16 on the way (of `normed`, `queries`, `key_proj`, `values`, `weights`, `attended`, `mixed_rows` and `activated`) count: a program that leaves them out, or rounds other values in their place, can miss the bound.
Values may be sent and summed in bfloat16 or wider, within the bound.
A program may use at most 64 MiB of HBM per device.

```python
import math
import jax
import jax.numpy as jnp
from jax import lax

CHAN = 512
FRAMES = 64
VIDEOS = 1
FRAMES_OUT = 32
HEIGHT = 32
WIDTH = 512


def pair_weights(key):
    base = jax.random.fold_in(key, 7)
    first_key, second_key = jax.random.split(base, 2)
    scale = CHAN ** (-0.5)
    first = jnp.clip(jax.random.normal(first_key, (CHAN, CHAN), jnp.float32), -6.0, 6.0) * scale
    second = jnp.clip(jax.random.normal(second_key, (CHAN, CHAN), jnp.float32), -6.0, 6.0) * scale
    return (first, second)


def draw_w_query(key, part):
    return pair_weights(key)[0].astype(jnp.bfloat16)


def draw_w_key(key, part):
    return pair_weights(key)[1].astype(jnp.bfloat16)


def level_of(own_key, dims, pieces, low, high):
    loudness = 1.0
    for position, parts in pieces:
        heights = jax.random.uniform(jax.random.fold_in(jax.random.fold_in(own_key, 6), position), (parts,), jnp.float32, low / len(pieces), high / len(pieces))
        loudness = loudness * jnp.repeat(jnp.exp(heights), dims[position] // parts).reshape((-1,) + (1,) * (len(dims) - 1 - position))
    return loudness


def centred(stream_key, shape, width, bound, pieces=(), dtype=jnp.bfloat16):
    level = level_of(stream_key, shape, pieces, -0.22, 0.18) if pieces else 1.0
    entries = jax.random.normal(stream_key, shape, jnp.float32) * width * level
    return jnp.minimum(jnp.maximum(entries, -bound), bound).astype(dtype)


def setup_inputs(seed: int = 0) -> dict:
    streams_of = jax.random.split(jax.random.key(seed), 9)
    video = centred(streams_of[0], (VIDEOS * FRAMES, HEIGHT, WIDTH, CHAN), 1.0, 6.0, ((0, 32), (2, 16)))
    norm_gain = jnp.clip(1.0 + 0.15 * jax.random.normal(streams_of[1], (CHAN,), jnp.float32), 0.25, 1.75)
    w_query = draw_w_query(jax.random.fold_in(streams_of[8], 71), 0)
    w_key = draw_w_key(jax.random.fold_in(streams_of[8], 71), 0)
    w_value = centred(streams_of[4], (CHAN, CHAN), CHAN ** -0.5, 0.25)
    w_out = centred(streams_of[5], (CHAN, CHAN), CHAN ** -0.5, 0.25)
    w_time = centred(streams_of[6], (3, CHAN, CHAN), (3 * CHAN) ** -0.5, 0.15625)
    w_depth = centred(streams_of[7], (3, 3, CHAN), 9 ** -0.5, 2.0, (), jnp.float32)
    return dict(video=video, norm_gain=norm_gain, w_query=w_query, w_key=w_key, w_value=w_value, w_out=w_out, w_time=w_time, w_depth=w_depth)


epsilon = 1e-06

def attend_row(row_slab, norm_gain, w_query, w_key, w_value, w_out):
    channels = row_slab.shape[-1]
    widened = row_slab.reshape(-1, channels).astype(jnp.float32)
    normed = (widened * lax.rsqrt(lax.optimization_barrier(jnp.mean(widened * widened, axis=-1, keepdims=True)) + epsilon) * norm_gain).astype(jnp.bfloat16)
    grid_shape = (VIDEOS, FRAMES, -1, channels)
    queries = jnp.dot(normed, w_query, preferred_element_type=jnp.float32).astype(jnp.bfloat16).reshape(grid_shape)
    key_proj = jnp.dot(normed, w_key, preferred_element_type=jnp.float32).astype(jnp.bfloat16).reshape(grid_shape)
    values = jnp.dot(normed, w_value, preferred_element_type=jnp.float32).astype(jnp.bfloat16).reshape(grid_shape)
    scores = jnp.einsum('bqpc,bkpc->bpqk', queries.astype(jnp.float32), key_proj.astype(jnp.float32)) / math.sqrt(channels)
    causal = jnp.arange(FRAMES)[:, None] >= jnp.arange(FRAMES)[None, :]
    scores = jnp.where(causal, scores, -1e+30)
    raised = jnp.exp(scores - lax.optimization_barrier(jnp.max(scores, axis=-1, keepdims=True)))
    weights = (raised / lax.optimization_barrier(jnp.sum(raised, axis=-1, keepdims=True))).astype(jnp.bfloat16)
    attended = jnp.einsum('bpqk,bkpc->bqpc', weights.astype(jnp.float32), values.astype(jnp.float32)).astype(jnp.bfloat16)
    projected = jnp.dot(attended.reshape(-1, channels), w_out, preferred_element_type=jnp.float32)
    return (widened + projected).astype(jnp.bfloat16).reshape(row_slab.shape)

def time_conv(prior_frames, even_frames, odd_frames, w_time):
    channels = even_frames.shape[-1]
    summed = jnp.dot(prior_frames.reshape(-1, channels), w_time[0], preferred_element_type=jnp.float32)
    summed = summed + jnp.dot(even_frames.reshape(-1, channels), w_time[1], preferred_element_type=jnp.float32)
    summed = summed + jnp.dot(odd_frames.reshape(-1, channels), w_time[2], preferred_element_type=jnp.float32)
    return jax.nn.silu(summed).astype(jnp.bfloat16).reshape(even_frames.shape)

def reference(video, norm_gain, w_query, w_key, w_value, w_out, w_time, w_depth):
    channels = video.shape[-1]
    rows_first = jnp.moveaxis(video, 1, 0)

    def per_row(row_slab):
        mixed_rows = attend_row(row_slab, norm_gain, w_query, w_key, w_value, w_out)
        grouped = mixed_rows.reshape(VIDEOS, FRAMES, -1, channels)
        even_frames = grouped[:, 0::2]
        odd_frames = grouped[:, 1::2]
        prior_frames = jnp.concatenate([grouped[:, :1], odd_frames[:, :-1]], axis=1)
        return time_conv(prior_frames, even_frames, odd_frames, w_time).reshape(VIDEOS * FRAMES_OUT, -1, channels)
    activated = jnp.moveaxis(lax.map(per_row, rows_first), 0, 1)

    def per_frame(frame):
        rows = frame.shape[0]
        cols = frame.shape[1]
        padded = jnp.pad(frame.astype(jnp.float32), ((1, 1), (1, 1), (0, 0)))
        summed = jnp.zeros(frame.shape, jnp.float32)
        for row_step in range(3):
            for col_step in range(3):
                summed = summed + padded[row_step:row_step + rows, col_step:col_step + cols] * w_depth[row_step, col_step]
        return summed.astype(jnp.bfloat16)
    return lax.map(per_frame, activated)
```

```python
import math

import jax
import jax.numpy as jnp
from jax import lax
from jax.sharding import PartitionSpec as P

FRAMES = 64
VIDEOS = 1


epsilon = 1e-06


def padded_2(block, sides, width):
    for axis, dim in sides:
        count = lax.axis_size(axis)
        forward = [(i, i + 1) for i in range(count - 1)]
        backward = [(target, source) for source, target in forward]
        low = lax.ppermute(
            lax.slice_in_dim(block, block.shape[dim] - width, None, axis=dim), axis, forward
        )
        high = lax.ppermute(lax.slice_in_dim(block, 0, width, axis=dim), axis, backward)
        block = jnp.concatenate([low, block, high], axis=dim)
    return block


def attend_block(block_in, norm_gain, w_query, w_key, w_value, w_out):
    channels = block_in.shape[-1]
    widened = block_in.reshape(-1, channels).astype(jnp.float32)
    normed = (
        widened
        * lax.rsqrt(jnp.mean(widened * widened, axis=-1, keepdims=True) + epsilon)
        * norm_gain
    ).astype(jnp.bfloat16)
    grid_shape = (VIDEOS, FRAMES, -1, channels)
    queries = (
        jnp.dot(normed, w_query, preferred_element_type=jnp.float32)
        .astype(jnp.bfloat16)
        .reshape(grid_shape)
    )
    key_proj = (
        jnp.dot(normed, w_key, preferred_element_type=jnp.float32)
        .astype(jnp.bfloat16)
        .reshape(grid_shape)
    )
    values = (
        jnp.dot(normed, w_value, preferred_element_type=jnp.float32)
        .astype(jnp.bfloat16)
        .reshape(grid_shape)
    )
    scores = jnp.einsum(
        "bqpc,bkpc->bpqk", queries, key_proj, preferred_element_type=jnp.float32
    ) / math.sqrt(channels)
    causal = jnp.arange(FRAMES)[:, None] >= jnp.arange(FRAMES)[None, :]
    scores = jnp.where(causal, scores, -1e30)
    raised = jnp.exp(scores - jnp.max(scores, axis=-1, keepdims=True))
    weights = (raised / jnp.sum(raised, axis=-1, keepdims=True)).astype(jnp.bfloat16)
    attended = jnp.einsum(
        "bpqk,bkpc->bqpc", weights, values, preferred_element_type=jnp.float32
    ).astype(jnp.bfloat16)
    projected = jnp.dot(attended.reshape(-1, channels), w_out, preferred_element_type=jnp.float32)
    return (widened + projected).astype(jnp.bfloat16).reshape(block_in.shape)


def time_conv(prior_frames, even_frames, odd_frames, w_time):
    channels = even_frames.shape[-1]
    summed = jnp.dot(
        prior_frames.reshape(-1, channels), w_time[0], preferred_element_type=jnp.float32
    )
    summed = summed + jnp.dot(
        even_frames.reshape(-1, channels), w_time[1], preferred_element_type=jnp.float32
    )
    summed = summed + jnp.dot(
        odd_frames.reshape(-1, channels), w_time[2], preferred_element_type=jnp.float32
    )
    return jax.nn.silu(summed).astype(jnp.bfloat16).reshape(even_frames.shape)


def local(video, norm_gain, w_query, w_key, w_value, w_out, w_time, w_depth):
    mixed_rows = attend_block(
        lax.all_to_all(video, "frm", split_axis=1, concat_axis=0, tiled=True),
        norm_gain,
        w_query,
        w_key,
        w_value,
        w_out,
    )
    even_frames = mixed_rows[0::2]
    odd_frames = mixed_rows[1::2]
    prior_frames = jnp.concatenate([mixed_rows[:1], odd_frames[:-1]], axis=0)
    mixed_time = time_conv(prior_frames, even_frames, odd_frames, w_time)
    activated = lax.all_to_all(mixed_time, "frm", split_axis=0, concat_axis=1, tiled=True)
    rimmed = padded_2(activated, (("col", 2),), 1)
    rows = activated.shape[1]
    cols = activated.shape[2]
    padded = jnp.pad(rimmed.astype(jnp.float32), ((0, 0), (1, 1), (0, 0), (0, 0)))
    summed = jnp.zeros(activated.shape, jnp.float32)
    for row_step in range(3):
        for col_step in range(3):
            summed = (
                summed
                + padded[:, row_step : row_step + rows, col_step : col_step + cols]
                * w_depth[row_step, col_step]
            )
    return summed.astype(jnp.bfloat16)


def solution(mesh):
    return jax.shard_map(
        local,
        mesh=mesh,
        in_specs=(P("frm", None, "col", None), P(), P(), P(), P(), P(), P(), P()),
        out_specs=P("frm", None, "col", None),
        check_vma=False,
    )
```

```python
import functools
import math

import jax
import jax.numpy as jnp
from jax import lax
from jax.experimental import pallas as pl
from jax.experimental.pallas import tpu as pltpu
from jax.sharding import PartitionSpec as P

MESH = pl.DeviceIdType.MESH
EPSILON = 1e-06
BLOCK = 8


def attend(slab, gain, w_query, w_key, w_value, w_out):
    rows, channels = slab.shape
    scale = lax.rsqrt(jnp.mean(slab * slab, axis=-1, keepdims=True) + EPSILON)
    normed = (slab * scale * gain).astype(jnp.bfloat16)
    queries = jnp.dot(normed, w_query, preferred_element_type=jnp.float32).astype(jnp.bfloat16)
    key_proj = jnp.dot(normed, w_key, preferred_element_type=jnp.float32).astype(jnp.bfloat16)
    values = jnp.dot(normed, w_value, preferred_element_type=jnp.float32).astype(jnp.bfloat16)
    scores = lax.dot_general(
        queries, key_proj, (((1,), (1,)), ((), ())), preferred_element_type=jnp.float32
    ) * (1.0 / math.sqrt(channels))
    ahead = lax.broadcasted_iota(jnp.int32, (rows, rows), 0) - lax.broadcasted_iota(
        jnp.int32, (rows, rows), 1
    )
    seen = (ahead >= 0) & ((ahead & (BLOCK - 1)) == 0)
    scores = jnp.where(seen, scores, -1e30)
    raised = jnp.exp(scores - jnp.max(scores, axis=-1, keepdims=True))
    weights = (raised / jnp.sum(raised, axis=-1, keepdims=True)).astype(jnp.bfloat16)
    attended = jnp.dot(weights, values, preferred_element_type=jnp.float32).astype(jnp.bfloat16)
    return slab + jnp.dot(attended, w_out, preferred_element_type=jnp.float32)


def time_conv(mixed, w_time):
    rows, channels = mixed.shape
    pairs = mixed.reshape(rows // (2 * BLOCK), 2 * BLOCK, channels)
    even = pairs[:, :BLOCK].reshape(rows // 2, channels)
    odd = pairs[:, BLOCK:].reshape(rows // 2, channels)
    prior = jnp.concatenate([even[:BLOCK], odd[:-BLOCK]], axis=0)
    summed = jnp.dot(prior.astype(jnp.bfloat16), w_time[0], preferred_element_type=jnp.float32)
    summed += jnp.dot(even.astype(jnp.bfloat16), w_time[1], preferred_element_type=jnp.float32)
    summed += jnp.dot(odd.astype(jnp.bfloat16), w_time[2], preferred_element_type=jnp.float32)
    return summed / (1.0 + jnp.exp(-summed))


def kernel(
    n,
    n_col,
    video,
    gain,
    w_query,
    w_key,
    w_value,
    w_out,
    w_time,
    w_depth,
    out,
    slabs,
    acts,
    frame,
    low_rim,
    high_rim,
    wq,
    wk,
    wv,
    wo,
    wt,
    taps,
    weight_sem,
    own_sem,
    slab_send,
    slab_recv,
    own_act_sem,
    act_send,
    act_recv,
    rim_send,
    rim_recv,
):
    me = lax.axis_index("frm")
    col = lax.axis_index("col")
    chunks, frames, _, channels = slabs.shape
    chips = n // 2
    rows = n
    chip, core = me // 2, me % 2

    weights = [
        pltpu.make_async_copy(source, target, weight_sem.at[i])
        for i, (source, target) in enumerate(
            ((w_query, wq), (w_key, wk), (w_value, wv), (w_out, wo), (w_time, wt))
        )
    ]
    for copy in weights:
        copy.start()

    barrier = pltpu.get_barrier_semaphore()

    @pl.loop(1, n)
    def _(step):
        pl.semaphore_signal(
            barrier, inc=1, device_id={"frm": (me + step) % n}, device_id_type=MESH
        )

    right, left = (col + 1) % n_col, (col + n_col - 1) % n_col
    for neighbour in (left, right):
        pl.semaphore_signal(barrier, inc=1, device_id={"col": neighbour}, device_id_type=MESH)

    for edge in (0, rows + 1):
        frame[:, edge] = jnp.zeros((chunks, BLOCK, channels), frame.dtype)
    for tap in range(9):
        taps[tap] = jnp.broadcast_to(w_depth[pl.ds(tap, 1), :], (BLOCK, channels))

    def columns(step):
        return pl.ds(pl.multiple_of((step * (chunks - 1)) % chunks * BLOCK, BLOCK), BLOCK)

    def own_slab(step):
        return pltpu.make_async_copy(
            video.at[:, me, columns(step)], slabs.at[step, pl.ds(2 * me, 2)], own_sem.at[step]
        )

    for step in range(chunks):
        own_slab(step).start()

    pl.semaphore_wait(barrier, n - 1 + 2)

    def partner(turn):
        hop, other = (turn + 1) // 2, (turn + 1) % 2
        away = (hop + 1) // 2
        signed = away * (2 * (hop % 2) - 1)
        return (chip + signed + chips) % chips * 2 + (core + other) % 2

    def send_slab(step, turn):
        to = partner(turn)
        pltpu.make_async_remote_copy(
            src_ref=video.at[:, to, columns(step)],
            dst_ref=slabs.at[step, pl.ds(2 * me, 2)],
            send_sem=slab_send,
            recv_sem=slab_recv.at[step],
            device_id={"frm": to},
            device_id_type=MESH,
        ).start()

    @pl.loop(0, chunks)
    def _(step):
        @pl.loop(0, n - 1)
        def _(turn):
            send_slab(step, turn)

    for copy in weights:
        copy.wait()

    @pl.loop(0, chunks)
    def _(step):
        own_slab(step).wait()
        arrived = slabs.at[step, pl.ds(0, frames - 2)]
        pltpu.make_async_copy(arrived, arrived, slab_recv.at[step]).wait()
        slab = slabs[step].astype(jnp.float32).reshape(frames * BLOCK, channels)
        mixed = attend(slab, gain[...], wq[...], wk[...], wv[...], wo[...])
        activated = time_conv(mixed, wt)
        acts[step] = activated.reshape(rows, BLOCK, channels).astype(acts.dtype)
        pltpu.make_async_copy(
            acts.at[step, me], frame.at[step, me + 1], own_act_sem.at[step]
        ).start()

        @pl.loop(0, n - 1)
        def _(turn):
            to = partner(n - 2 - turn)
            pltpu.make_async_remote_copy(
                src_ref=acts.at[step, to],
                dst_ref=frame.at[step, me + 1],
                send_sem=act_send,
                recv_sem=act_recv.at[step],
                device_id={"frm": to},
                device_id_type=MESH,
            ).start()

    def wait_frame(step):
        pltpu.make_async_copy(
            acts.at[step, me], frame.at[step, me + 1], own_act_sem.at[step]
        ).wait()
        arrived = frame.at[step, pl.ds(0, rows - 1)]
        pltpu.make_async_copy(arrived, arrived, act_recv.at[step]).wait()

    wait_frame(0)
    to_left = pltpu.make_async_remote_copy(
        src_ref=frame.at[0],
        dst_ref=high_rim,
        send_sem=rim_send.at[0],
        recv_sem=rim_recv.at[0],
        device_id={"col": left},
        device_id_type=MESH,
    )
    to_left.start()
    wait_frame(1)
    to_right = pltpu.make_async_remote_copy(
        src_ref=frame.at[1],
        dst_ref=low_rim,
        send_sem=rim_send.at[1],
        recv_sem=rim_recv.at[1],
        device_id={"col": right},
        device_id_type=MESH,
    )
    to_right.start()
    for step in range(2, chunks):
        wait_frame(step)
    to_left.wait()
    to_right.wait()

    has_left = jnp.where(col > 0, 1.0, 0.0)
    has_right = jnp.where(col < n_col - 1, 1.0, 0.0)
    width = chunks * BLOCK
    lanes = 256
    order = [(chunks - block) % chunks for block in range(chunks)]

    @pl.loop(0, rows)
    def _(row):
        for lane in range(0, channels, lanes):
            span = pl.ds(lane, lanes)
            sums = [None, None, None]
            low = high = None
            for a in range(3):
                line = jnp.concatenate(
                    [frame[chunk, row + a, :, span].astype(jnp.float32) for chunk in order], axis=0
                )
                line = line.reshape(chunks, BLOCK, lanes)
                for b in range(3):
                    term = line * taps[3 * a + b, :, span]
                    sums[b] = term if a == 0 else sums[b] + term
                below = low_rim[row + a, :, span].astype(jnp.float32) * taps[3 * a, :, span]
                above = high_rim[row + a, :, span].astype(jnp.float32) * taps[3 * a + 2, :, span]
                low = below if a == 0 else low + below
                high = above if a == 0 else high + above
            place = lax.broadcasted_iota(jnp.int32, (width, lanes), 0)
            before = pltpu.roll(sums[0].reshape(width, lanes), 1, 0)
            after = pltpu.roll(sums[2].reshape(width, lanes), width - 1, 0)
            low = jnp.where(has_left > 0.0, low[BLOCK - 1 :], 0.0)
            high = jnp.where(has_right > 0.0, high[:1], 0.0)
            before = jnp.where(place == 0, low, before)
            after = jnp.where(place == width - 1, high, after)
            total = before + sums[1].reshape(width, lanes) + after
            out[0, row, :, span] = total.astype(out.dtype)

    sent = slabs.at[:, pl.ds(0, frames - 2)]
    pltpu.make_async_copy(sent, sent, slab_send).wait()
    sent = acts.at[:, pl.ds(0, rows - 1)]
    pltpu.make_async_copy(sent, sent, act_send).wait()


def solution(mesh):
    n, n_col = mesh.shape["frm"], mesh.shape["col"]

    def local(video, norm_gain, w_query, w_key, w_value, w_out, w_time, w_depth):
        own, rows, cols, channels = video.shape
        chunks = cols // BLOCK
        any_space = pl.BlockSpec(memory_space=pl.ANY)
        vmem = pl.BlockSpec(memory_space=pltpu.VMEM)
        square = pltpu.VMEM((channels, channels), jnp.bfloat16)
        dma = pltpu.SemaphoreType.DMA
        return pl.pallas_call(
            functools.partial(kernel, n, n_col),
            out_shape=jax.ShapeDtypeStruct((1, rows, cols, channels), jnp.bfloat16),
            in_specs=[any_space, vmem] + [any_space] * 5 + [vmem],
            out_specs=vmem,
            scratch_shapes=[
                pltpu.VMEM((chunks, own * n, BLOCK, channels), jnp.bfloat16),
                pltpu.VMEM((chunks, n, BLOCK, channels), jnp.bfloat16),
                pltpu.VMEM((chunks, rows + 2, BLOCK, channels), jnp.bfloat16),
                pltpu.VMEM((rows + 2, BLOCK, channels), jnp.bfloat16),
                pltpu.VMEM((rows + 2, BLOCK, channels), jnp.bfloat16),
                square,
                square,
                square,
                square,
                pltpu.VMEM((3, channels, channels), jnp.bfloat16),
                pltpu.VMEM((9, BLOCK, channels), jnp.float32),
                dma((5,)),
                dma((chunks,)),
                dma,
                dma((chunks,)),
                dma((chunks,)),
                dma,
                dma((chunks,)),
                dma((2,)),
                dma((2,)),
            ],
            compiler_params=pltpu.CompilerParams(collective_id=0, has_side_effects=True),
        )(
            video,
            norm_gain.reshape(1, channels),
            w_query,
            w_key,
            w_value,
            w_out,
            w_time,
            w_depth.reshape(9, channels),
        )

    return jax.shard_map(
        local,
        mesh=mesh,
        in_specs=(P("frm", None, "col", None), P(), P(), P(), P(), P(), P(), P()),
        out_specs=P("frm", None, "col", None),
        check_vma=False,
    )
```

```python
import functools
import math

import jax
import jax.numpy as jnp
from jax import lax
from jax.experimental import pallas as pl
from jax.experimental.pallas import tpu as pltpu
from jax.sharding import PartitionSpec as P

MESH = pl.DeviceIdType.MESH
EPSILON = 1e-06
BLOCK = 8
NEAR = 2
LANES = 128
GROUP = 4


def attend(slab, gain, w_query, w_key, w_value, w_out):
    rows, channels = slab.shape
    scale = lax.rsqrt(jnp.mean(slab * slab, axis=-1, keepdims=True) + EPSILON)
    normed = (slab * scale * gain).astype(jnp.bfloat16)
    queries = jnp.dot(normed, w_query, preferred_element_type=jnp.float32).astype(jnp.bfloat16)
    key_proj = jnp.dot(normed, w_key, preferred_element_type=jnp.float32).astype(jnp.bfloat16)
    values = jnp.dot(normed, w_value, preferred_element_type=jnp.float32).astype(jnp.bfloat16)
    scores = lax.dot_general(
        queries, key_proj, (((1,), (1,)), ((), ())), preferred_element_type=jnp.float32
    ) * (1.0 / math.sqrt(channels))
    ahead = lax.broadcasted_iota(jnp.int32, (rows, rows), 0) - lax.broadcasted_iota(
        jnp.int32, (rows, rows), 1
    )
    seen = (ahead >= 0) & ((ahead & (BLOCK - 1)) == 0)
    scores = jnp.where(seen, scores, -1e30)
    raised = jnp.exp(scores - jnp.max(scores, axis=-1, keepdims=True))
    weights = (raised / jnp.sum(raised, axis=-1, keepdims=True)).astype(jnp.bfloat16)
    attended = jnp.dot(weights, values, preferred_element_type=jnp.float32).astype(jnp.bfloat16)
    return slab + jnp.dot(attended, w_out, preferred_element_type=jnp.float32)


def time_conv(mixed, w_time):
    rows, channels = mixed.shape
    pairs = mixed.reshape(rows // (2 * BLOCK), 2 * BLOCK, channels)
    even = pairs[:, :BLOCK].reshape(rows // 2, channels)
    odd = pairs[:, BLOCK:].reshape(rows // 2, channels)
    prior = jnp.concatenate([even[:BLOCK], odd[:-BLOCK]], axis=0)
    summed = jnp.dot(prior.astype(jnp.bfloat16), w_time[0], preferred_element_type=jnp.float32)
    summed += jnp.dot(even.astype(jnp.bfloat16), w_time[1], preferred_element_type=jnp.float32)
    summed += jnp.dot(odd.astype(jnp.bfloat16), w_time[2], preferred_element_type=jnp.float32)
    return summed / (1.0 + jnp.exp(-summed))


def exchange(
    n,
    n_col,
    video,
    gain,
    w_query,
    w_key,
    w_value,
    w_out,
    w_time,
    frame,
    low_rim,
    high_rim,
    slabs,
    acts,
    wq,
    wk,
    wv,
    wo,
    wt,
    weight_sem,
    own_sem,
    slab_send,
    slab_recv,
    own_act_sem,
    act_send,
    act_recv,
    rim_send,
    rim_recv,
    right_known,
    left_known,
):
    me = lax.axis_index("frm")
    col = lax.axis_index("col")
    chunks, frames, _, channels = slabs.shape
    chips = n // 2
    rows = n
    chip, core = me // 2, me % 2
    far = chips // 2

    weights = [
        pltpu.make_async_copy(source, target, weight_sem.at[i])
        for i, (source, target) in enumerate(
            ((w_query, wq), (w_key, wk), (w_value, wv), (w_out, wo), (w_time, wt))
        )
    ]

    def device(away, other):
        return (chip + away + chips) % chips * 2 + (core + other) % 2

    barrier = pltpu.get_barrier_semaphore()
    for away in (1, -1):
        for other in (0, 1):
            pl.semaphore_signal(
                barrier, inc=1, device_id={"frm": device(away, other)}, device_id_type=MESH
            )
    pl.semaphore_signal(barrier, inc=1, device_id={"frm": device(0, 1)}, device_id_type=MESH)
    right, left = (col + 1) % n_col, (col + n_col - 1) % n_col
    for neighbour in (left, right):
        pl.semaphore_signal(barrier, inc=1, device_id={"col": neighbour}, device_id_type=MESH)

    def columns(step):
        return pl.ds(pl.multiple_of((step * (chunks - 1)) % chunks * BLOCK, BLOCK), BLOCK)

    def own_slab(step):
        return pltpu.make_async_copy(
            video.at[:, me, columns(step)], slabs.at[step, pl.ds(2 * me, 2)], own_sem.at[step]
        )

    for copy in weights:
        copy.start()
    for step in range(chunks):
        own_slab(step).start()

    pl.semaphore_wait(barrier, 7)

    def send_slab(step, to):
        pltpu.make_async_remote_copy(
            src_ref=video.at[:, to, columns(step)],
            dst_ref=slabs.at[step, pl.ds(2 * me, 2)],
            send_sem=slab_send,
            recv_sem=slab_recv.at[step],
            device_id={"frm": to},
            device_id_type=MESH,
        ).start()

    def send_slabs(first, last, away):
        @pl.loop(first, last)
        def _(step):
            for side in (1, -1) if away < far else (1,):
                for other in (0, 1):
                    send_slab(step, device(side * away, other))

    for away in range(1, far + 1):
        for side, known, reach in ((1, right_known, far), (-1, left_known, far - 1)):
            if 1 < away <= reach:
                pl.semaphore_wait(known.at[away], 1)
            if away < reach:
                pl.semaphore_signal(
                    known.at[away + 1],
                    inc=1,
                    device_id={"frm": device(-side, 0)},
                    device_id_type=MESH,
                )
        send_slabs(0, chunks if away <= NEAR else 1, away)
        if away == 1:

            @pl.loop(0, chunks)
            def _(step):
                send_slab(step, device(0, 1))

    @pl.loop(1, chunks)
    def _(step):
        @pl.loop(NEAR + 1, far)
        def _(away):
            for side in (1, -1):
                for other in (0, 1):
                    send_slab(step, device(side * away, other))

        for other in (0, 1):
            send_slab(step, device(far, other))

    for copy in weights:
        copy.wait()

    def partner(turn):
        hop, other = (turn + 1) // 2, (turn + 1) % 2
        return device((hop + 1) // 2 * (2 * (hop % 2) - 1), other)

    def own_act(step):
        return pltpu.make_async_copy(
            acts.at[step, me], frame.at[me, columns(step)], own_act_sem.at[step]
        )

    @pl.loop(0, chunks)
    def _(step):
        own_slab(step).wait()
        arrived = slabs.at[step, pl.ds(0, frames - 2)]
        pltpu.make_async_copy(arrived, arrived, slab_recv.at[step]).wait()
        slab = slabs[step].astype(jnp.float32).reshape(frames * BLOCK, channels)
        mixed = attend(slab, gain[...], wq[...], wk[...], wv[...], wo[...])
        activated = time_conv(mixed, wt)
        acts[step] = activated.reshape(rows, BLOCK, channels).astype(acts.dtype)
        own_act(step).start()

        @pl.loop(0, n - 1)
        def _(turn):
            to = partner(n - 2 - turn)
            pltpu.make_async_remote_copy(
                src_ref=acts.at[step, to],
                dst_ref=frame.at[me, columns(step)],
                send_sem=act_send,
                recv_sem=act_recv.at[step],
                device_id={"frm": to},
                device_id_type=MESH,
            ).start()

    def wait_frame(step):
        own_act(step).wait()
        arrived = frame.at[pl.ds(0, rows - 1), columns(step)]
        pltpu.make_async_copy(arrived, arrived, act_recv.at[step]).wait()

    def rim(step, target, neighbour):
        return pltpu.make_async_remote_copy(
            src_ref=frame.at[:, columns(step)],
            dst_ref=target,
            send_sem=rim_send.at[step],
            recv_sem=rim_recv.at[step],
            device_id={"col": neighbour},
            device_id_type=MESH,
        )

    to_left, to_right = rim(0, high_rim, left), rim(1, low_rim, right)
    wait_frame(0)
    to_left.start()
    wait_frame(1)
    to_right.start()
    for step in range(2, chunks):
        wait_frame(step)
    to_left.wait()
    to_right.wait()

    sent = slabs.at[:, pl.ds(0, frames - 2)]
    pltpu.make_async_copy(sent, sent, slab_send).wait()
    sent = acts.at[:, pl.ds(0, rows - 1)]
    pltpu.make_async_copy(sent, sent, act_send).wait()


def depthwise(n_col, frame, low_rim, high_rim, w_depth, out, image, low, high, result, sems, out_sems):
    col = lax.axis_index("col")
    rows, width, channels = frame.shape
    tiles = channels // LANES

    def loads(tile):
        span = pl.ds(tile * LANES, LANES)
        inside = pl.ds(1, rows)
        return [
            pltpu.make_async_copy(
                source.at[:, :, span], target.at[inside, :, span], sems.at[tile, i]
            )
            for i, (source, target) in enumerate(((frame, image), (low_rim, low), (high_rim, high)))
        ]

    def store(tile):
        span = pl.ds(tile * LANES, LANES)
        return pltpu.make_async_copy(
            result.at[:, :, span], out.at[0, :, :, span], out_sems.at[tile]
        )

    for tile in range(tiles):
        for copy in loads(tile):
            copy.start()
    for target in (image, low, high):
        for edge in (0, rows + 1):
            target[edge] = jnp.zeros(target.shape[1:], target.dtype)
    has_left, has_right = col > 0, col < n_col - 1
    place = lax.broadcasted_iota(jnp.int32, (width, LANES), 0)

    for tile in range(tiles):
        for copy in loads(tile):
            copy.wait()
        span = pl.ds(tile * LANES, LANES)
        taps = [[w_depth[a, pl.ds(b, 1), span] for b in range(3)] for a in range(3)]

        @pl.loop(0, rows // GROUP)
        def _(group):
            row = group * GROUP
            lines = [image[row + a, :, span].astype(jnp.float32) for a in range(GROUP + 2)]
            lows = [low[row + a, :, span].astype(jnp.float32) for a in range(GROUP + 2)]
            highs = [high[row + a, :, span].astype(jnp.float32) for a in range(GROUP + 2)]

            def column_sum(values, r, b):
                return values[r] * taps[0][b] + values[r + 1] * taps[1][b] + values[r + 2] * taps[2][b]

            for r in range(GROUP):
                before = pltpu.roll(column_sum(lines, r, 0), 1, 0)
                after = pltpu.roll(column_sum(lines, r, 2), width - 1, 0)
                first = jnp.where(has_left, column_sum(lows, r, 0)[BLOCK - 1 :], 0.0)
                last = jnp.where(has_right, column_sum(highs, r, 2)[:1], 0.0)
                total = jnp.where(place == 0, first, before) + column_sum(lines, r, 1)
                total += jnp.where(place == width - 1, last, after)
                result[row + r, :, span] = total.astype(result.dtype)

        store(tile).start()
    for tile in range(tiles):
        store(tile).wait()


def solution(mesh):
    n, n_col = mesh.shape["frm"], mesh.shape["col"]

    def local(video, norm_gain, w_query, w_key, w_value, w_out, w_time, w_depth):
        own, rows, cols, channels = video.shape
        chunks = cols // BLOCK
        half = n // 4
        any_space = pl.BlockSpec(memory_space=pl.ANY)
        vmem = pl.BlockSpec(memory_space=pltpu.VMEM)
        square = pltpu.VMEM((channels, channels), jnp.bfloat16)
        dma = pltpu.SemaphoreType.DMA
        rim = jax.ShapeDtypeStruct((rows, BLOCK, channels), jnp.bfloat16)
        frame, low_rim, high_rim = pl.pallas_call(
            functools.partial(exchange, n, n_col),
            out_shape=(jax.ShapeDtypeStruct((rows, cols, channels), jnp.bfloat16), rim, rim),
            in_specs=[any_space, vmem] + [any_space] * 5,
            out_specs=[any_space] * 3,
            scratch_shapes=[
                pltpu.VMEM((chunks, own * n, BLOCK, channels), jnp.bfloat16),
                pltpu.VMEM((chunks, n, BLOCK, channels), jnp.bfloat16),
                square,
                square,
                square,
                square,
                pltpu.VMEM((3, channels, channels), jnp.bfloat16),
                dma((5,)),
                dma((chunks,)),
                dma,
                dma((chunks,)),
                dma((chunks,)),
                dma,
                dma((chunks,)),
                dma((2,)),
                dma((2,)),
                pltpu.SemaphoreType.REGULAR((half + 1,)),
                pltpu.SemaphoreType.REGULAR((half + 1,)),
            ],
            compiler_params=pltpu.CompilerParams(collective_id=0, has_side_effects=True),
        )(video, norm_gain.reshape(1, channels), w_query, w_key, w_value, w_out, w_time)
        tiles = channels // LANES
        return pl.pallas_call(
            functools.partial(depthwise, n_col),
            out_shape=jax.ShapeDtypeStruct((1, rows, cols, channels), jnp.bfloat16),
            in_specs=[any_space] * 3 + [vmem],
            out_specs=any_space,
            scratch_shapes=[
                pltpu.VMEM((rows + 2, cols, channels), jnp.bfloat16),
                pltpu.VMEM((rows + 2, BLOCK, channels), jnp.bfloat16),
                pltpu.VMEM((rows + 2, BLOCK, channels), jnp.bfloat16),
                pltpu.VMEM((rows, cols, channels), jnp.bfloat16),
                dma((tiles, 3)),
                dma((tiles,)),
            ],
        )(frame, low_rim, high_rim, w_depth)

    return jax.shard_map(
        local,
        mesh=mesh,
        in_specs=(P("frm", None, "col", None), P(), P(), P(), P(), P(), P(), P()),
        out_specs=P("frm", None, "col", None),
        check_vma=False,
    )
```

```python
import functools
import math

import jax
import jax.numpy as jnp
from jax import lax
from jax.experimental import pallas as pl
from jax.experimental.pallas import tpu as pltpu
from jax.sharding import PartitionSpec as P

MESH = pl.DeviceIdType.MESH
EPSILON = 1e-06
BLOCK = 8
NEAR = 2
LANES = 256
PIECES = 4


def attend(slab, gain, w_query, w_key, w_value, w_out):
    rows, channels = slab.shape
    scale = lax.rsqrt(jnp.mean(slab * slab, axis=-1, keepdims=True) + EPSILON)
    normed = (slab * scale * gain).astype(jnp.bfloat16)
    queries = jnp.dot(normed, w_query, preferred_element_type=jnp.float32).astype(jnp.bfloat16)
    key_proj = jnp.dot(normed, w_key, preferred_element_type=jnp.float32).astype(jnp.bfloat16)
    values = jnp.dot(normed, w_value, preferred_element_type=jnp.float32).astype(jnp.bfloat16)
    scores = lax.dot_general(
        queries, key_proj, (((1,), (1,)), ((), ())), preferred_element_type=jnp.float32
    ) * (1.0 / math.sqrt(channels))
    ahead = lax.broadcasted_iota(jnp.int32, (rows, rows), 0) - lax.broadcasted_iota(
        jnp.int32, (rows, rows), 1
    )
    seen = (ahead >= 0) & ((ahead & (BLOCK - 1)) == 0)
    scores = jnp.where(seen, scores, -1e30)
    raised = jnp.exp(scores - jnp.max(scores, axis=-1, keepdims=True))
    weights = (raised / jnp.sum(raised, axis=-1, keepdims=True)).astype(jnp.bfloat16)
    attended = jnp.dot(weights, values, preferred_element_type=jnp.float32).astype(jnp.bfloat16)
    return slab + jnp.dot(attended, w_out, preferred_element_type=jnp.float32)


def time_conv(mixed, w_time):
    rows, channels = mixed.shape
    pairs = mixed.reshape(rows // (2 * BLOCK), 2 * BLOCK, channels)
    even = pairs[:, :BLOCK].reshape(rows // 2, channels)
    odd = pairs[:, BLOCK:].reshape(rows // 2, channels)
    prior = jnp.concatenate([even[:BLOCK], odd[:-BLOCK]], axis=0)
    summed = jnp.dot(prior.astype(jnp.bfloat16), w_time[0], preferred_element_type=jnp.float32)
    summed += jnp.dot(even.astype(jnp.bfloat16), w_time[1], preferred_element_type=jnp.float32)
    summed += jnp.dot(odd.astype(jnp.bfloat16), w_time[2], preferred_element_type=jnp.float32)
    return summed / (1.0 + jnp.exp(-summed))


def exchange(
    n,
    n_col,
    video,
    gain,
    w_query,
    w_key,
    w_value,
    w_out,
    w_time,
    w_depth,
    done,
    middle,
    edges,
    slabs,
    acts,
    frame,
    low_rim,
    high_rim,
    filtered,
    partial,
    wq,
    wk,
    wv,
    wo,
    wt,
    weight_sem,
    own_sem,
    slab_send,
    slab_recv,
    own_act_sem,
    act_send,
    act_recv,
    rim_send,
    rim_recv,
    done_sem,
    right_known,
    left_known,
):
    me = lax.axis_index("frm")
    col = lax.axis_index("col")
    chunks, frames, _, channels = slabs.shape
    chips = n // 2
    rows = n
    chip, core = me // 2, me % 2
    far = chips // 2

    weights = [
        pltpu.make_async_copy(source, target, weight_sem.at[i])
        for i, (source, target) in enumerate(
            ((w_query, wq), (w_key, wk), (w_value, wv), (w_out, wo), (w_time, wt))
        )
    ]

    def device(away, other):
        return (chip + away + chips) % chips * 2 + (core + other) % 2

    barrier = pltpu.get_barrier_semaphore()
    for away in (1, -1):
        for other in (0, 1):
            pl.semaphore_signal(
                barrier, inc=1, device_id={"frm": device(away, other)}, device_id_type=MESH
            )
    pl.semaphore_signal(barrier, inc=1, device_id={"frm": device(0, 1)}, device_id_type=MESH)
    right, left = (col + 1) % n_col, (col + n_col - 1) % n_col
    for neighbour in (left, right):
        pl.semaphore_signal(barrier, inc=1, device_id={"col": neighbour}, device_id_type=MESH)

    def columns(step):
        return pl.ds(pl.multiple_of((step * (chunks - 1)) % chunks * BLOCK, BLOCK), BLOCK)

    def own_slab(step):
        return pltpu.make_async_copy(
            video.at[:, me, columns(step)], slabs.at[step, pl.ds(2 * me, 2)], own_sem.at[step]
        )

    for copy in weights:
        copy.start()
    for step in range(chunks):
        own_slab(step).start()

    pl.semaphore_wait(barrier, 7)

    def send_slab(step, to):
        pltpu.make_async_remote_copy(
            src_ref=video.at[:, to, columns(step)],
            dst_ref=slabs.at[step, pl.ds(2 * me, 2)],
            send_sem=slab_send,
            recv_sem=slab_recv.at[step],
            device_id={"frm": to},
            device_id_type=MESH,
        ).start()

    def send_slabs(first, last, away):
        @pl.loop(first, last)
        def _(step):
            for side in (1, -1) if away < far else (1,):
                for other in (0, 1):
                    send_slab(step, device(side * away, other))

    for away in range(1, far + 1):
        for side, known, reach in ((1, right_known, far), (-1, left_known, far - 1)):
            if 1 < away <= reach:
                pl.semaphore_wait(known.at[away], 1)
            if away < reach:
                pl.semaphore_signal(
                    known.at[away + 1],
                    inc=1,
                    device_id={"frm": device(-side, 0)},
                    device_id_type=MESH,
                )
        send_slabs(0, chunks if away <= NEAR else 1, away)
        if away == 1:

            @pl.loop(0, chunks)
            def _(step):
                send_slab(step, device(0, 1))

    @pl.loop(1, chunks)
    def _(step):
        @pl.loop(NEAR + 1, far)
        def _(away):
            for side in (1, -1):
                for other in (0, 1):
                    send_slab(step, device(side * away, other))

        for other in (0, 1):
            send_slab(step, device(far, other))

    for copy in weights:
        copy.wait()

    def partner(turn):
        hop, other = (turn + 1) // 2, (turn + 1) % 2
        return device((hop + 1) // 2 * (2 * (hop % 2) - 1), other)

    def landing(step, row):
        return middle.at[row] if step == chunks - 1 else frame.at[step, row + 1]

    def own_act(step):
        return pltpu.make_async_copy(acts.at[step, me], landing(step, me), own_act_sem.at[step])

    def send_acts(step, recv_step, target):
        @pl.loop(0, n - 1)
        def _(turn):
            to = partner(n - 2 - turn)
            pltpu.make_async_remote_copy(
                src_ref=acts.at[step, to],
                dst_ref=target,
                send_sem=act_send,
                recv_sem=act_recv.at[recv_step],
                device_id={"frm": to},
                device_id_type=MESH,
            ).start()

    for edge in (0, rows + 1):
        frame[:, edge] = jnp.zeros((chunks - 1, BLOCK, channels), frame.dtype)

    @pl.loop(0, chunks)
    def _(step):
        own_slab(step).wait()
        arrived = slabs.at[step, pl.ds(0, frames - 2)]
        pltpu.make_async_copy(arrived, arrived, slab_recv.at[step]).wait()
        slab = slabs[step].astype(jnp.float32).reshape(frames * BLOCK, channels)
        mixed = attend(slab, gain[...], wq[...], wk[...], wv[...], wo[...])
        activated = time_conv(mixed, wt)
        acts[step] = activated.reshape(rows, BLOCK, channels).astype(acts.dtype)

        @pl.when(step < chunks - 1)
        def _():
            pltpu.make_async_copy(
                acts.at[step, me], frame.at[step, me + 1], own_act_sem.at[step]
            ).start()
            send_acts(step, step, frame.at[step, me + 1])

        @pl.when(step == chunks - 1)
        def _():
            own_act(chunks - 1).start()
            send_acts(chunks - 1, chunks - 1, middle.at[me])

    def wait_frame(step):
        own_act(step).wait()
        ref = middle if step == chunks - 1 else frame.at[step]
        arrived = ref.at[pl.ds(0, rows - 1)]
        pltpu.make_async_copy(arrived, arrived, act_recv.at[step]).wait()

    def rim(step, target, neighbour):
        return pltpu.make_async_remote_copy(
            src_ref=frame.at[step],
            dst_ref=target,
            send_sem=rim_send.at[step],
            recv_sem=rim_recv.at[step],
            device_id={"col": neighbour},
            device_id_type=MESH,
        )

    to_left, to_right = rim(0, high_rim, left), rim(1, low_rim, right)
    wait_frame(0)
    to_left.start()
    wait_frame(1)
    to_right.start()
    wait_frame(2)
    to_left.wait()
    to_right.wait()

    has_left, has_right = col > 0, col < n_col - 1
    place = lax.broadcasted_iota(jnp.int32, (BLOCK, LANES), 0)

    @pl.loop(0, rows)
    def _(row):
        for lane in range(0, channels, LANES):
            span = pl.ds(lane, LANES)

            def column_sum(ref, b):
                total = None
                for a in range(3):
                    term = ref[row + a, :, span].astype(jnp.float32) * w_depth[a, pl.ds(b, 1), span]
                    total = term if total is None else total + term
                return total

            first, third, fourth = frame.at[0], frame.at[2], frame.at[1]
            first_0, first_1, first_2 = (column_sum(first, b) for b in range(3))
            third_0, third_1, third_2 = (column_sum(third, b) for b in range(3))
            fourth_0, fourth_1, fourth_2 = (column_sum(fourth, b) for b in range(3))
            low = pltpu.roll(column_sum(low_rim, 0), 1, 0)
            high = pltpu.roll(column_sum(high_rim, 2), BLOCK - 1, 0)
            low = jnp.where(has_left, low, 0.0)
            high = jnp.where(has_right, high, 0.0)

            def before(own, previous):
                return jnp.where(place == 0, previous, pltpu.roll(own, 1, 0))

            def after(own, following):
                return jnp.where(place == BLOCK - 1, following, pltpu.roll(own, BLOCK - 1, 0))

            first_part = before(first_0, low) + first_1
            third_part = third_1 + after(third_2, pltpu.roll(fourth_2, BLOCK - 1, 0))
            fourth_part = before(fourth_0, pltpu.roll(third_0, 1, 0)) + fourth_1
            filtered[0, row, :, span] = (first_part + pltpu.roll(first_2, BLOCK - 1, 0)).astype(
                filtered.dtype
            )
            filtered[2, row, :, span] = (third_part + pltpu.roll(third_0, 1, 0)).astype(
                filtered.dtype
            )
            filtered[1, row, :, span] = (fourth_part + after(fourth_2, high)).astype(filtered.dtype)
            kept = jnp.where(place == 0, third_part, first_part)
            kept = jnp.where(place == 1, pltpu.roll(first_0, 2, 0), kept)
            kept = jnp.where(place == BLOCK - 2, pltpu.roll(third_2, BLOCK - 2, 0), kept)
            partial[row, :, span] = kept

    stores = [
        pltpu.make_async_copy(
            filtered.at[step], done.at[:, columns(step)], done_sem.at[step]
        )
        for step in range(chunks - 1)
    ]
    stores.append(pltpu.make_async_copy(partial, edges, done_sem.at[chunks - 1]))
    for copy in stores:
        copy.start()
    for copy in stores:
        copy.wait()
    sent = slabs.at[:, pl.ds(0, frames - 2)]
    pltpu.make_async_copy(sent, sent, slab_send).wait()
    wait_frame(chunks - 1)
    sent = acts.at[:, pl.ds(0, rows - 1)]
    pltpu.make_async_copy(sent, sent, act_send).wait()


def finish(done, middle, edges, w_depth, out, image, inner, partial, sems, out_sems):
    rows, width, channels = done.shape
    band = rows // PIECES

    def load(piece, i):
        here = pl.ds(piece * band, band)
        if i == 0:
            source, target = middle.at[here], inner.at[pl.ds(piece * band + 1, band)]
        elif i == 1:
            source, target = edges.at[here], partial.at[here]
        else:
            span = pl.ds(0, BLOCK) if i == 2 else pl.ds(2 * BLOCK, 2 * BLOCK)
            source, target = done.at[here, span], image.at[here, span]
        return pltpu.make_async_copy(source, target, sems.at[piece, i])

    def store(piece):
        here = pl.ds(piece * band, band)
        return pltpu.make_async_copy(image.at[here], out.at[0, here], out_sems.at[piece])

    for piece in range(PIECES):
        for i in range(4):
            load(piece, i).start()
    for edge in (0, rows + 1):
        inner[edge] = jnp.zeros(inner.shape[1:], inner.dtype)
    place = lax.broadcasted_iota(jnp.int32, (BLOCK, LANES), 0)

    for piece in range(PIECES):
        for i in range(1 if piece else 0, 4):
            load(piece, i).wait()
        if piece + 1 < PIECES:
            load(piece + 1, 0).wait()

        @pl.loop(piece * band, (piece + 1) * band)
        def _(row):
            for lane in range(0, channels, LANES):
                span = pl.ds(lane, LANES)
                lines = [inner[row + a, :, span].astype(jnp.float32) for a in range(3)]
                sums = []
                for b in range(3):
                    total = lines[0] * w_depth[0, pl.ds(b, 1), span]
                    for a in (1, 2):
                        total += lines[a] * w_depth[a, pl.ds(b, 1), span]
                    sums.append(total)
                kept = partial[row, :, span]
                before = pltpu.roll(sums[0], 1, 0)
                after = pltpu.roll(sums[2], BLOCK - 1, 0)
                total = sums[1] + jnp.where(place == 0, pltpu.roll(kept, BLOCK - 1, 0), before)
                total += jnp.where(place == BLOCK - 1, pltpu.roll(kept, 1, 0), after)
                first, third = pl.ds(0, BLOCK), pl.ds(2 * BLOCK, BLOCK)
                image[row, pl.ds(BLOCK, BLOCK), span] = total.astype(image.dtype)
                value = image[row, first, span].astype(jnp.float32)
                value = jnp.where(place == BLOCK - 1, kept + after, value)
                image[row, first, span] = value.astype(image.dtype)
                value = image[row, third, span].astype(jnp.float32)
                value = jnp.where(place == 0, kept + before, value)
                image[row, third, span] = value.astype(image.dtype)

        store(piece).start()
    for piece in range(PIECES):
        store(piece).wait()


def solution(mesh):
    n, n_col = mesh.shape["frm"], mesh.shape["col"]

    def local(video, norm_gain, w_query, w_key, w_value, w_out, w_time, w_depth):
        own, rows, cols, channels = video.shape
        chunks = cols // BLOCK
        half = n // 4
        any_space = pl.BlockSpec(memory_space=pl.ANY)
        vmem = pl.BlockSpec(memory_space=pltpu.VMEM)
        square = pltpu.VMEM((channels, channels), jnp.bfloat16)
        dma = pltpu.SemaphoreType.DMA
        block = pltpu.VMEM((rows + 2, BLOCK, channels), jnp.bfloat16)
        done, middle, edges = pl.pallas_call(
            functools.partial(exchange, n, n_col),
            out_shape=(
                jax.ShapeDtypeStruct((rows, cols, channels), jnp.bfloat16),
                jax.ShapeDtypeStruct((rows, BLOCK, channels), jnp.bfloat16),
                jax.ShapeDtypeStruct((rows, BLOCK, channels), jnp.float32),
            ),
            in_specs=[any_space, vmem] + [any_space] * 5 + [vmem],
            out_specs=[any_space] * 3,
            scratch_shapes=[
                pltpu.VMEM((chunks, own * n, BLOCK, channels), jnp.bfloat16),
                pltpu.VMEM((chunks, n, BLOCK, channels), jnp.bfloat16),
                pltpu.VMEM((chunks - 1, rows + 2, BLOCK, channels), jnp.bfloat16),
                block,
                block,
                pltpu.VMEM((chunks - 1, rows, BLOCK, channels), jnp.bfloat16),
                pltpu.VMEM((rows, BLOCK, channels), jnp.float32),
                square,
                square,
                square,
                square,
                pltpu.VMEM((3, channels, channels), jnp.bfloat16),
                dma((5,)),
                dma((chunks,)),
                dma,
                dma((chunks,)),
                dma((chunks,)),
                dma,
                dma((chunks,)),
                dma((2,)),
                dma((2,)),
                dma((chunks,)),
                pltpu.SemaphoreType.REGULAR((half + 1,)),
                pltpu.SemaphoreType.REGULAR((half + 1,)),
            ],
            compiler_params=pltpu.CompilerParams(collective_id=0, has_side_effects=True),
        )(video, norm_gain.reshape(1, channels), w_query, w_key, w_value, w_out, w_time, w_depth)
        return pl.pallas_call(
            finish,
            out_shape=jax.ShapeDtypeStruct((1, rows, cols, channels), jnp.bfloat16),
            in_specs=[any_space] * 3 + [vmem],
            out_specs=any_space,
            scratch_shapes=[
                pltpu.VMEM((rows, cols, channels), jnp.bfloat16),
                block,
                pltpu.VMEM((rows, BLOCK, channels), jnp.float32),
                dma((PIECES, 4)),
                dma((PIECES,)),
            ],
        )(done, middle, edges, w_depth)

    return jax.shard_map(
        local,
        mesh=mesh,
        in_specs=(P("frm", None, "col", None), P(), P(), P(), P(), P(), P(), P()),
        out_specs=P("frm", None, "col", None),
        check_vma=False,
    )
```

```python
import functools
import math

import jax
import jax.numpy as jnp
from jax import lax
from jax.experimental import pallas as pl
from jax.experimental.pallas import tpu as pltpu
from jax.sharding import PartitionSpec as P

MESH = pl.DeviceIdType.MESH
EPSILON = 1e-06
BLOCK = 8
NEAR = 2
LANES = 256
PIECES = 4


def attend(slab, gain, w_query, w_key, w_value, w_out):
    rows, channels = slab.shape
    scale = lax.rsqrt(jnp.mean(slab * slab, axis=-1, keepdims=True) + EPSILON)
    normed = (slab * scale * gain).astype(jnp.bfloat16)
    queries = jnp.dot(normed, w_query, preferred_element_type=jnp.float32).astype(jnp.bfloat16)
    key_proj = jnp.dot(normed, w_key, preferred_element_type=jnp.float32).astype(jnp.bfloat16)
    values = jnp.dot(normed, w_value, preferred_element_type=jnp.float32).astype(jnp.bfloat16)
    scores = lax.dot_general(
        queries, key_proj, (((1,), (1,)), ((), ())), preferred_element_type=jnp.float32
    ) * (1.0 / math.sqrt(channels))
    ahead = lax.broadcasted_iota(jnp.int32, (rows, rows), 0) - lax.broadcasted_iota(
        jnp.int32, (rows, rows), 1
    )
    seen = (ahead >= 0) & ((ahead & (BLOCK - 1)) == 0)
    scores = jnp.where(seen, scores, -1e30)
    raised = jnp.exp(scores - jnp.max(scores, axis=-1, keepdims=True))
    weights = (raised / jnp.sum(raised, axis=-1, keepdims=True)).astype(jnp.bfloat16)
    attended = jnp.dot(weights, values, preferred_element_type=jnp.float32).astype(jnp.bfloat16)
    return slab + jnp.dot(attended, w_out, preferred_element_type=jnp.float32)


def time_conv(mixed, w_time):
    rows, channels = mixed.shape
    pairs = mixed.reshape(rows // (2 * BLOCK), 2 * BLOCK, channels)
    even = pairs[:, :BLOCK].reshape(rows // 2, channels)
    odd = pairs[:, BLOCK:].reshape(rows // 2, channels)
    prior = jnp.concatenate([even[:BLOCK], odd[:-BLOCK]], axis=0)
    summed = jnp.dot(prior.astype(jnp.bfloat16), w_time[0], preferred_element_type=jnp.float32)
    summed += jnp.dot(even.astype(jnp.bfloat16), w_time[1], preferred_element_type=jnp.float32)
    summed += jnp.dot(odd.astype(jnp.bfloat16), w_time[2], preferred_element_type=jnp.float32)
    return summed / (1.0 + jnp.exp(-summed))


def exchange(
    n,
    n_col,
    video,
    gain_in,
    w_query,
    w_key,
    w_value,
    w_out,
    w_time,
    w_depth_in,
    done,
    middle,
    edges,
    slabs,
    acts,
    frame,
    low_rim,
    high_rim,
    filtered,
    partial,
    wq,
    wk,
    wv,
    wo,
    wt,
    gain,
    w_depth,
    weight_sem,
    own_sem,
    slab_send,
    slab_recv,
    own_act_sem,
    act_send,
    act_recv,
    rim_send,
    rim_recv,
    done_sem,
    right_known,
    left_known,
):
    me = lax.axis_index("frm")
    col = lax.axis_index("col")
    chunks, frames, _, channels = slabs.shape
    chips = n // 2
    rows = n
    chip, core = me // 2, me % 2
    far = chips // 2

    weights = [
        pltpu.make_async_copy(source, target, weight_sem.at[i])
        for i, (source, target) in enumerate(
            (
                (w_query, wq),
                (w_key, wk),
                (w_value, wv),
                (w_out, wo),
                (w_time, wt),
                (gain_in, gain),
                (w_depth_in, w_depth),
            )
        )
    ]

    def device(away, other):
        return (chip + away + chips) % chips * 2 + (core + other) % 2

    barrier = pltpu.get_barrier_semaphore()
    for away in (1, -1):
        for other in (0, 1):
            pl.semaphore_signal(
                barrier, inc=1, device_id={"frm": device(away, other)}, device_id_type=MESH
            )
    pl.semaphore_signal(barrier, inc=1, device_id={"frm": device(0, 1)}, device_id_type=MESH)
    right, left = (col + 1) % n_col, (col + n_col - 1) % n_col
    for neighbour in (left, right):
        pl.semaphore_signal(barrier, inc=1, device_id={"col": neighbour}, device_id_type=MESH)

    def columns(step):
        return pl.ds(pl.multiple_of((step * (chunks - 1)) % chunks * BLOCK, BLOCK), BLOCK)

    def own_slab(step):
        return pltpu.make_async_copy(
            video.at[:, me, columns(step)], slabs.at[step, pl.ds(2 * me, 2)], own_sem.at[step]
        )

    for copy in weights:
        copy.start()
    for step in range(chunks):
        own_slab(step).start()

    pl.semaphore_wait(barrier, 7)

    def send_slab(step, to):
        pltpu.make_async_remote_copy(
            src_ref=video.at[:, to, columns(step)],
            dst_ref=slabs.at[step, pl.ds(2 * me, 2)],
            send_sem=slab_send,
            recv_sem=slab_recv.at[step],
            device_id={"frm": to},
            device_id_type=MESH,
        ).start()

    def send_slabs(first, last, away):
        @pl.loop(first, last)
        def _(step):
            for side in (1, -1) if away < far else (1,):
                for other in (0, 1):
                    send_slab(step, device(side * away, other))

    for away in range(1, far + 1):
        for side, known, reach in ((1, right_known, far), (-1, left_known, far - 1)):
            if 1 < away <= reach:
                pl.semaphore_wait(known.at[away], 1)
            if away < reach:
                pl.semaphore_signal(
                    known.at[away + 1],
                    inc=1,
                    device_id={"frm": device(-side, 0)},
                    device_id_type=MESH,
                )
        send_slabs(0, chunks if away <= NEAR else 1, away)
        if away == 1:

            @pl.loop(0, chunks)
            def _(step):
                send_slab(step, device(0, 1))

    @pl.loop(1, chunks)
    def _(step):
        @pl.loop(NEAR + 1, far)
        def _(away):
            for side in (1, -1):
                for other in (0, 1):
                    send_slab(step, device(side * away, other))

        for other in (0, 1):
            send_slab(step, device(far, other))

    for copy in weights:
        copy.wait()

    def partner(turn):
        hop, other = (turn + 1) // 2, (turn + 1) % 2
        return device((hop + 1) // 2 * (2 * (hop % 2) - 1), other)

    def landing(step, row):
        return middle.at[row] if step == chunks - 1 else frame.at[step, row + 1]

    def own_act(step):
        return pltpu.make_async_copy(acts.at[step, me], landing(step, me), own_act_sem.at[step])

    def send_acts(step, recv_step, target):
        @pl.loop(0, n - 1)
        def _(turn):
            to = partner(n - 2 - turn)
            pltpu.make_async_remote_copy(
                src_ref=acts.at[step, to],
                dst_ref=target,
                send_sem=act_send,
                recv_sem=act_recv.at[recv_step],
                device_id={"frm": to},
                device_id_type=MESH,
            ).start()

    for edge in (0, rows + 1):
        frame[:, edge] = jnp.zeros((chunks - 1, BLOCK, channels), frame.dtype)

    @pl.loop(0, chunks)
    def _(step):
        own_slab(step).wait()
        arrived = slabs.at[step, pl.ds(0, frames - 2)]
        pltpu.make_async_copy(arrived, arrived, slab_recv.at[step]).wait()
        slab = slabs[step].astype(jnp.float32).reshape(frames * BLOCK, channels)
        mixed = attend(slab, gain[...], wq[...], wk[...], wv[...], wo[...])
        activated = time_conv(mixed, wt)
        acts[step] = activated.reshape(rows, BLOCK, channels).astype(acts.dtype)

        @pl.when(step < chunks - 1)
        def _():
            pltpu.make_async_copy(
                acts.at[step, me], frame.at[step, me + 1], own_act_sem.at[step]
            ).start()
            send_acts(step, step, frame.at[step, me + 1])

        @pl.when(step == chunks - 1)
        def _():
            own_act(chunks - 1).start()
            send_acts(chunks - 1, chunks - 1, middle.at[me])

    def wait_frame(step):
        own_act(step).wait()
        ref = middle if step == chunks - 1 else frame.at[step]
        arrived = ref.at[pl.ds(0, rows - 1)]
        pltpu.make_async_copy(arrived, arrived, act_recv.at[step]).wait()

    def rim(step, target, neighbour):
        return pltpu.make_async_remote_copy(
            src_ref=frame.at[step],
            dst_ref=target,
            send_sem=rim_send.at[step],
            recv_sem=rim_recv.at[step],
            device_id={"col": neighbour},
            device_id_type=MESH,
        )

    to_left, to_right = rim(0, high_rim, left), rim(1, low_rim, right)
    wait_frame(0)
    to_left.start()
    wait_frame(1)
    to_right.start()
    wait_frame(2)
    to_left.wait()
    to_right.wait()

    has_left, has_right = col > 0, col < n_col - 1
    place = lax.broadcasted_iota(jnp.int32, (BLOCK, LANES), 0)

    @pl.loop(0, rows)
    def _(row):
        for lane in range(0, channels, LANES):
            span = pl.ds(lane, LANES)

            def column_sum(ref, b):
                total = None
                for a in range(3):
                    term = ref[row + a, :, span].astype(jnp.float32) * w_depth[a, pl.ds(b, 1), span]
                    total = term if total is None else total + term
                return total

            first, third, fourth = frame.at[0], frame.at[2], frame.at[1]
            first_0, first_1, first_2 = (column_sum(first, b) for b in range(3))
            third_0, third_1, third_2 = (column_sum(third, b) for b in range(3))
            fourth_0, fourth_1, fourth_2 = (column_sum(fourth, b) for b in range(3))
            low = pltpu.roll(column_sum(low_rim, 0), 1, 0)
            high = pltpu.roll(column_sum(high_rim, 2), BLOCK - 1, 0)
            low = jnp.where(has_left, low, 0.0)
            high = jnp.where(has_right, high, 0.0)

            def before(own, previous):
                return jnp.where(place == 0, previous, pltpu.roll(own, 1, 0))

            def after(own, following):
                return jnp.where(place == BLOCK - 1, following, pltpu.roll(own, BLOCK - 1, 0))

            first_part = before(first_0, low) + first_1
            third_part = third_1 + after(third_2, pltpu.roll(fourth_2, BLOCK - 1, 0))
            fourth_part = before(fourth_0, pltpu.roll(third_0, 1, 0)) + fourth_1
            filtered[0, row, :, span] = (first_part + pltpu.roll(first_2, BLOCK - 1, 0)).astype(
                filtered.dtype
            )
            filtered[2, row, :, span] = (third_part + pltpu.roll(third_0, 1, 0)).astype(
                filtered.dtype
            )
            filtered[1, row, :, span] = (fourth_part + after(fourth_2, high)).astype(filtered.dtype)
            kept = jnp.where(place == 0, third_part, first_part)
            kept = jnp.where(place == 1, pltpu.roll(first_0, 2, 0), kept)
            kept = jnp.where(place == BLOCK - 2, pltpu.roll(third_2, BLOCK - 2, 0), kept)
            partial[row, :, span] = kept

    stores = [
        pltpu.make_async_copy(
            filtered.at[step], done.at[:, columns(step)], done_sem.at[step]
        )
        for step in range(chunks - 1)
    ]
    stores.append(pltpu.make_async_copy(partial, edges, done_sem.at[chunks - 1]))
    for copy in stores:
        copy.start()
    for copy in stores:
        copy.wait()
    sent = slabs.at[:, pl.ds(0, frames - 2)]
    pltpu.make_async_copy(sent, sent, slab_send).wait()
    wait_frame(chunks - 1)
    sent = acts.at[:, pl.ds(0, rows - 1)]
    pltpu.make_async_copy(sent, sent, act_send).wait()


def finish(
    done, middle, edges, w_depth_in, out, image, inner, partial, w_depth, sems, out_sems, taps_sem
):
    rows, width, channels = done.shape
    band = rows // PIECES

    def load(piece, i):
        here = pl.ds(piece * band, band)
        if i == 0:
            source, target = middle.at[here], inner.at[pl.ds(piece * band + 1, band)]
        elif i == 1:
            source, target = edges.at[here], partial.at[here]
        else:
            span = pl.ds(0, BLOCK) if i == 2 else pl.ds(2 * BLOCK, 2 * BLOCK)
            source, target = done.at[here, span], image.at[here, span]
        return pltpu.make_async_copy(source, target, sems.at[piece, i])

    def store(piece):
        here = pl.ds(piece * band, band)
        return pltpu.make_async_copy(image.at[here], out.at[0, here], out_sems.at[piece])

    for piece in range(PIECES):
        for i in range(4):
            load(piece, i).start()
        if piece == 0:
            taps = pltpu.make_async_copy(w_depth_in, w_depth, taps_sem)
            taps.start()
    for edge in (0, rows + 1):
        inner[edge] = jnp.zeros(inner.shape[1:], inner.dtype)
    place = lax.broadcasted_iota(jnp.int32, (BLOCK, LANES), 0)

    taps.wait()
    for piece in range(PIECES):
        for i in range(1 if piece else 0, 4):
            load(piece, i).wait()
        if piece + 1 < PIECES:
            load(piece + 1, 0).wait()

        @pl.loop(piece * band, (piece + 1) * band)
        def _(row):
            for lane in range(0, channels, LANES):
                span = pl.ds(lane, LANES)
                lines = [inner[row + a, :, span].astype(jnp.float32) for a in range(3)]
                sums = []
                for b in range(3):
                    total = lines[0] * w_depth[0, pl.ds(b, 1), span]
                    for a in (1, 2):
                        total += lines[a] * w_depth[a, pl.ds(b, 1), span]
                    sums.append(total)
                kept = partial[row, :, span]
                before = pltpu.roll(sums[0], 1, 0)
                after = pltpu.roll(sums[2], BLOCK - 1, 0)
                total = sums[1] + jnp.where(place == 0, pltpu.roll(kept, BLOCK - 1, 0), before)
                total += jnp.where(place == BLOCK - 1, pltpu.roll(kept, 1, 0), after)
                first, third = pl.ds(0, BLOCK), pl.ds(2 * BLOCK, BLOCK)
                image[row, pl.ds(BLOCK, BLOCK), span] = total.astype(image.dtype)
                value = image[row, first, span].astype(jnp.float32)
                value = jnp.where(place == BLOCK - 1, kept + after, value)
                image[row, first, span] = value.astype(image.dtype)
                value = image[row, third, span].astype(jnp.float32)
                value = jnp.where(place == 0, kept + before, value)
                image[row, third, span] = value.astype(image.dtype)

        store(piece).start()
    for piece in range(PIECES):
        store(piece).wait()


def solution(mesh):
    n, n_col = mesh.shape["frm"], mesh.shape["col"]

    def local(video, norm_gain, w_query, w_key, w_value, w_out, w_time, w_depth):
        own, rows, cols, channels = video.shape
        chunks = cols // BLOCK
        half = n // 4
        any_space = pl.BlockSpec(memory_space=pl.ANY)
        square = pltpu.VMEM((channels, channels), jnp.bfloat16)
        dma = pltpu.SemaphoreType.DMA
        block = pltpu.VMEM((rows + 2, BLOCK, channels), jnp.bfloat16)
        done, middle, edges = pl.pallas_call(
            functools.partial(exchange, n, n_col),
            out_shape=(
                jax.ShapeDtypeStruct((rows, cols, channels), jnp.bfloat16),
                jax.ShapeDtypeStruct((rows, BLOCK, channels), jnp.bfloat16),
                jax.ShapeDtypeStruct((rows, BLOCK, channels), jnp.float32),
            ),
            in_specs=[any_space] * 8,
            out_specs=[any_space] * 3,
            scratch_shapes=[
                pltpu.VMEM((chunks, own * n, BLOCK, channels), jnp.bfloat16),
                pltpu.VMEM((chunks, n, BLOCK, channels), jnp.bfloat16),
                pltpu.VMEM((chunks - 1, rows + 2, BLOCK, channels), jnp.bfloat16),
                block,
                block,
                pltpu.VMEM((chunks - 1, rows, BLOCK, channels), jnp.bfloat16),
                pltpu.VMEM((rows, BLOCK, channels), jnp.float32),
                square,
                square,
                square,
                square,
                pltpu.VMEM((3, channels, channels), jnp.bfloat16),
                pltpu.VMEM((1, channels), jnp.float32),
                pltpu.VMEM(w_depth.shape, jnp.float32),
                dma((7,)),
                dma((chunks,)),
                dma,
                dma((chunks,)),
                dma((chunks,)),
                dma,
                dma((chunks,)),
                dma((2,)),
                dma((2,)),
                dma((chunks,)),
                pltpu.SemaphoreType.REGULAR((half + 1,)),
                pltpu.SemaphoreType.REGULAR((half + 1,)),
            ],
            compiler_params=pltpu.CompilerParams(collective_id=0, has_side_effects=True),
        )(video, norm_gain.reshape(1, channels), w_query, w_key, w_value, w_out, w_time, w_depth)
        return pl.pallas_call(
            finish,
            out_shape=jax.ShapeDtypeStruct((1, rows, cols, channels), jnp.bfloat16),
            in_specs=[any_space] * 4,
            out_specs=any_space,
            scratch_shapes=[
                pltpu.VMEM((rows, cols, channels), jnp.bfloat16),
                block,
                pltpu.VMEM((rows, BLOCK, channels), jnp.float32),
                pltpu.VMEM(w_depth.shape, jnp.float32),
                dma((PIECES, 4)),
                dma((PIECES,)),
                dma,
            ],
        )(done, middle, edges, w_depth)

    return jax.shard_map(
        local,
        mesh=mesh,
        in_specs=(P("frm", None, "col", None), P(), P(), P(), P(), P(), P(), P()),
        out_specs=P("frm", None, "col", None),
        check_vma=False,
    )
```

```python
import functools
import math

import jax
import jax.numpy as jnp
from jax import lax
from jax.experimental import pallas as pl
from jax.experimental.pallas import tpu as pltpu
from jax.sharding import PartitionSpec as P

MESH = pl.DeviceIdType.MESH
EPSILON = 1e-06
BLOCK = 8
NEAR = 2
LANES = 256
PIECES = 8


def attend(slab, gain, w_query, w_key, w_value, w_out):
    rows, channels = slab.shape
    scale = lax.rsqrt(jnp.mean(slab * slab, axis=-1, keepdims=True) + EPSILON)
    normed = (slab * scale * gain).astype(jnp.bfloat16)
    queries = jnp.dot(normed, w_query, preferred_element_type=jnp.float32).astype(jnp.bfloat16)
    key_proj = jnp.dot(normed, w_key, preferred_element_type=jnp.float32).astype(jnp.bfloat16)
    values = jnp.dot(normed, w_value, preferred_element_type=jnp.float32).astype(jnp.bfloat16)
    scores = lax.dot_general(
        queries, key_proj, (((1,), (1,)), ((), ())), preferred_element_type=jnp.float32
    ) * (1.0 / math.sqrt(channels))
    ahead = lax.broadcasted_iota(jnp.int32, (rows, rows), 0) - lax.broadcasted_iota(
        jnp.int32, (rows, rows), 1
    )
    seen = (ahead >= 0) & ((ahead & (BLOCK - 1)) == 0)
    scores = jnp.where(seen, scores, -1e30)
    raised = jnp.exp(scores - jnp.max(scores, axis=-1, keepdims=True))
    weights = (raised / jnp.sum(raised, axis=-1, keepdims=True)).astype(jnp.bfloat16)
    attended = jnp.dot(weights, values, preferred_element_type=jnp.float32).astype(jnp.bfloat16)
    return slab + jnp.dot(attended, w_out, preferred_element_type=jnp.float32)


def time_conv(mixed, w_time):
    rows, channels = mixed.shape
    pairs = mixed.reshape(rows // (2 * BLOCK), 2 * BLOCK, channels)
    even = pairs[:, :BLOCK].reshape(rows // 2, channels)
    odd = pairs[:, BLOCK:].reshape(rows // 2, channels)
    prior = jnp.concatenate([even[:BLOCK], odd[:-BLOCK]], axis=0)
    summed = jnp.dot(prior.astype(jnp.bfloat16), w_time[0], preferred_element_type=jnp.float32)
    summed += jnp.dot(even.astype(jnp.bfloat16), w_time[1], preferred_element_type=jnp.float32)
    summed += jnp.dot(odd.astype(jnp.bfloat16), w_time[2], preferred_element_type=jnp.float32)
    return summed / (1.0 + jnp.exp(-summed))


def exchange(
    n,
    n_col,
    video,
    gain_in,
    w_query,
    w_key,
    w_value,
    w_out,
    w_time,
    w_depth_in,
    done,
    middle,
    edges,
    slabs,
    acts,
    frame,
    low_rim,
    high_rim,
    filtered,
    partial,
    wq,
    wk,
    wv,
    wo,
    wt,
    gain,
    w_depth,
    weight_sem,
    own_sem,
    slab_send,
    slab_recv,
    own_act_sem,
    act_send,
    act_recv,
    rim_send,
    rim_recv,
    done_sem,
    right_known,
    left_known,
):
    me = lax.axis_index("frm")
    col = lax.axis_index("col")
    chunks, frames, _, channels = slabs.shape
    chips = n // 2
    rows = n
    chip, core = me // 2, me % 2
    far = chips // 2

    weights = [
        pltpu.make_async_copy(source, target, weight_sem.at[i])
        for i, (source, target) in enumerate(
            (
                (w_query, wq),
                (w_key, wk),
                (w_value, wv),
                (w_out, wo),
                (w_time, wt),
                (gain_in, gain),
                (w_depth_in, w_depth),
            )
        )
    ]

    def device(away, other):
        return (chip + away + chips) % chips * 2 + (core + other) % 2

    barrier = pltpu.get_barrier_semaphore()
    for away in (1, -1):
        for other in (0, 1):
            pl.semaphore_signal(
                barrier, inc=1, device_id={"frm": device(away, other)}, device_id_type=MESH
            )
    pl.semaphore_signal(barrier, inc=1, device_id={"frm": device(0, 1)}, device_id_type=MESH)
    right, left = (col + 1) % n_col, (col + n_col - 1) % n_col
    for neighbour in (left, right):
        pl.semaphore_signal(barrier, inc=1, device_id={"col": neighbour}, device_id_type=MESH)

    def columns(step):
        return pl.ds(pl.multiple_of((step * (chunks - 1)) % chunks * BLOCK, BLOCK), BLOCK)

    def own_slab(step):
        return pltpu.make_async_copy(
            video.at[:, me, columns(step)], slabs.at[step, pl.ds(2 * me, 2)], own_sem.at[step]
        )

    for copy in weights:
        copy.start()
    for step in range(chunks):
        own_slab(step).start()

    pl.semaphore_wait(barrier, 7)

    def send_slab(step, to):
        pltpu.make_async_remote_copy(
            src_ref=video.at[:, to, columns(step)],
            dst_ref=slabs.at[step, pl.ds(2 * me, 2)],
            send_sem=slab_send,
            recv_sem=slab_recv.at[step],
            device_id={"frm": to},
            device_id_type=MESH,
        ).start()

    def send_slabs(first, last, away):
        @pl.loop(first, last)
        def _(step):
            for side in (1, -1) if away < far else (1,):
                for other in (0, 1):
                    send_slab(step, device(side * away, other))

    for away in range(1, far + 1):
        for side, known, reach in ((1, right_known, far), (-1, left_known, far - 1)):
            if 1 < away <= reach:
                pl.semaphore_wait(known.at[away], 1)
            if away < reach:
                pl.semaphore_signal(
                    known.at[away + 1],
                    inc=1,
                    device_id={"frm": device(-side, 0)},
                    device_id_type=MESH,
                )
        send_slabs(0, chunks if away <= NEAR else 1, away)
        if away == 1:

            @pl.loop(0, chunks)
            def _(step):
                send_slab(step, device(0, 1))

    @pl.loop(1, chunks)
    def _(step):
        @pl.loop(NEAR + 1, far)
        def _(away):
            for side in (1, -1):
                for other in (0, 1):
                    send_slab(step, device(side * away, other))

        for other in (0, 1):
            send_slab(step, device(far, other))

    for copy in weights:
        copy.wait()

    def partner(turn):
        hop, other = (turn + 1) // 2, (turn + 1) % 2
        return device((hop + 1) // 2 * (2 * (hop % 2) - 1), other)

    def landing(step, row):
        return middle.at[row] if step == chunks - 1 else frame.at[step, row + 1]

    def own_act(step):
        return pltpu.make_async_copy(acts.at[step, me], landing(step, me), own_act_sem.at[step])

    def send_acts(step, recv_step, target):
        @pl.loop(0, n - 1)
        def _(turn):
            to = partner(n - 2 - turn)
            pltpu.make_async_remote_copy(
                src_ref=acts.at[step, to],
                dst_ref=target,
                send_sem=act_send,
                recv_sem=act_recv.at[recv_step],
                device_id={"frm": to},
                device_id_type=MESH,
            ).start()

    for edge in (0, rows + 1):
        frame[:, edge] = jnp.zeros((chunks - 1, BLOCK, channels), frame.dtype)

    @pl.loop(0, chunks)
    def _(step):
        own_slab(step).wait()
        arrived = slabs.at[step, pl.ds(0, frames - 2)]
        pltpu.make_async_copy(arrived, arrived, slab_recv.at[step]).wait()
        slab = slabs[step].astype(jnp.float32).reshape(frames * BLOCK, channels)
        mixed = attend(slab, gain[...], wq[...], wk[...], wv[...], wo[...])
        activated = time_conv(mixed, wt)
        acts[step] = activated.reshape(rows, BLOCK, channels).astype(acts.dtype)

        @pl.when(step < chunks - 1)
        def _():
            pltpu.make_async_copy(
                acts.at[step, me], frame.at[step, me + 1], own_act_sem.at[step]
            ).start()
            send_acts(step, step, frame.at[step, me + 1])

        @pl.when(step == chunks - 1)
        def _():
            own_act(chunks - 1).start()
            send_acts(chunks - 1, chunks - 1, middle.at[me])

    def wait_frame(step):
        own_act(step).wait()
        ref = middle if step == chunks - 1 else frame.at[step]
        arrived = ref.at[pl.ds(0, rows - 1)]
        pltpu.make_async_copy(arrived, arrived, act_recv.at[step]).wait()

    def rim(step, target, neighbour):
        return pltpu.make_async_remote_copy(
            src_ref=frame.at[step],
            dst_ref=target,
            send_sem=rim_send.at[step],
            recv_sem=rim_recv.at[step],
            device_id={"col": neighbour},
            device_id_type=MESH,
        )

    to_left, to_right = rim(0, high_rim, left), rim(1, low_rim, right)
    wait_frame(0)
    to_left.start()
    wait_frame(1)
    to_right.start()
    wait_frame(2)
    to_left.wait()
    to_right.wait()

    has_left, has_right = col > 0, col < n_col - 1
    place = lax.broadcasted_iota(jnp.int32, (BLOCK, LANES), 0)

    @pl.loop(0, rows)
    def _(row):
        for lane in range(0, channels, LANES):
            span = pl.ds(lane, LANES)

            def column_sum(ref, b):
                total = None
                for a in range(3):
                    term = ref[row + a, :, span].astype(jnp.float32) * w_depth[a, pl.ds(b, 1), span]
                    total = term if total is None else total + term
                return total

            first, third, fourth = frame.at[0], frame.at[2], frame.at[1]
            first_0, first_1, first_2 = (column_sum(first, b) for b in range(3))
            third_0, third_1, third_2 = (column_sum(third, b) for b in range(3))
            fourth_0, fourth_1, fourth_2 = (column_sum(fourth, b) for b in range(3))
            low = pltpu.roll(column_sum(low_rim, 0), 1, 0)
            high = pltpu.roll(column_sum(high_rim, 2), BLOCK - 1, 0)
            low = jnp.where(has_left, low, 0.0)
            high = jnp.where(has_right, high, 0.0)

            def before(own, previous):
                return jnp.where(place == 0, previous, pltpu.roll(own, 1, 0))

            def after(own, following):
                return jnp.where(place == BLOCK - 1, following, pltpu.roll(own, BLOCK - 1, 0))

            first_part = before(first_0, low) + first_1
            third_part = third_1 + after(third_2, pltpu.roll(fourth_2, BLOCK - 1, 0))
            fourth_part = before(fourth_0, pltpu.roll(third_0, 1, 0)) + fourth_1
            filtered[0, row, :, span] = (first_part + pltpu.roll(first_2, BLOCK - 1, 0)).astype(
                filtered.dtype
            )
            filtered[2, row, :, span] = (third_part + pltpu.roll(third_0, 1, 0)).astype(
                filtered.dtype
            )
            filtered[1, row, :, span] = (fourth_part + after(fourth_2, high)).astype(filtered.dtype)
            kept = jnp.where(place == 0, third_part, first_part)
            kept = jnp.where(place == 1, pltpu.roll(first_0, 2, 0), kept)
            kept = jnp.where(place == BLOCK - 2, pltpu.roll(third_2, BLOCK - 2, 0), kept)
            partial[row, :, span] = kept

    stores = [
        pltpu.make_async_copy(
            filtered.at[step], done.at[:, columns(step)], done_sem.at[step]
        )
        for step in range(chunks - 1)
    ]
    stores.append(pltpu.make_async_copy(partial, edges, done_sem.at[chunks - 1]))
    for copy in stores:
        copy.start()
    for copy in stores:
        copy.wait()
    sent = slabs.at[:, pl.ds(0, frames - 2)]
    pltpu.make_async_copy(sent, sent, slab_send).wait()
    wait_frame(chunks - 1)
    sent = acts.at[:, pl.ds(0, rows - 1)]
    pltpu.make_async_copy(sent, sent, act_send).wait()


def finish(
    done, middle, edges, w_depth_in, out, image, inner, partial, w_depth, sems, out_sems, taps_sem
):
    rows, width, channels = done.shape
    band = rows // PIECES

    def load(piece, i):
        here = pl.ds(piece * band, band)
        if i == 0:
            source, target = middle.at[here], inner.at[pl.ds(piece * band + 1, band)]
        elif i == 1:
            source, target = edges.at[here], partial.at[here]
        else:
            span = pl.ds(0, BLOCK) if i == 2 else pl.ds(2 * BLOCK, 2 * BLOCK)
            source, target = done.at[here, span], image.at[here, span]
        return pltpu.make_async_copy(source, target, sems.at[piece, i])

    def store(piece):
        here = pl.ds(piece * band, band)
        return pltpu.make_async_copy(image.at[here], out.at[0, here], out_sems.at[piece])

    for piece in range(PIECES):
        for i in range(4):
            load(piece, i).start()
        if piece == 0:
            taps = pltpu.make_async_copy(w_depth_in, w_depth, taps_sem)
            taps.start()
    for edge in (0, rows + 1):
        inner[edge] = jnp.zeros(inner.shape[1:], inner.dtype)
    place = lax.broadcasted_iota(jnp.int32, (BLOCK, LANES), 0)

    taps.wait()
    for piece in range(PIECES):
        for i in range(1 if piece else 0, 4):
            load(piece, i).wait()
        if piece + 1 < PIECES:
            load(piece + 1, 0).wait()

        @pl.loop(piece * band, (piece + 1) * band)
        def _(row):
            for lane in range(0, channels, LANES):
                span = pl.ds(lane, LANES)
                lines = [inner[row + a, :, span].astype(jnp.float32) for a in range(3)]
                sums = []
                for b in range(3):
                    total = lines[0] * w_depth[0, pl.ds(b, 1), span]
                    for a in (1, 2):
                        total += lines[a] * w_depth[a, pl.ds(b, 1), span]
                    sums.append(total)
                kept = partial[row, :, span]
                before = pltpu.roll(sums[0], 1, 0)
                after = pltpu.roll(sums[2], BLOCK - 1, 0)
                total = sums[1] + jnp.where(place == 0, pltpu.roll(kept, BLOCK - 1, 0), before)
                total += jnp.where(place == BLOCK - 1, pltpu.roll(kept, 1, 0), after)
                first, third = pl.ds(0, BLOCK), pl.ds(2 * BLOCK, BLOCK)
                image[row, pl.ds(BLOCK, BLOCK), span] = total.astype(image.dtype)
                value = image[row, first, span].astype(jnp.float32)
                value = jnp.where(place == BLOCK - 1, kept + after, value)
                image[row, first, span] = value.astype(image.dtype)
                value = image[row, third, span].astype(jnp.float32)
                value = jnp.where(place == 0, kept + before, value)
                image[row, third, span] = value.astype(image.dtype)

        store(piece).start()
    for piece in range(PIECES):
        store(piece).wait()


def solution(mesh):
    n, n_col = mesh.shape["frm"], mesh.shape["col"]

    def local(video, norm_gain, w_query, w_key, w_value, w_out, w_time, w_depth):
        own, rows, cols, channels = video.shape
        chunks = cols // BLOCK
        half = n // 4
        any_space = pl.BlockSpec(memory_space=pl.ANY)
        square = pltpu.VMEM((channels, channels), jnp.bfloat16)
        dma = pltpu.SemaphoreType.DMA
        block = pltpu.VMEM((rows + 2, BLOCK, channels), jnp.bfloat16)
        done, middle, edges = pl.pallas_call(
            functools.partial(exchange, n, n_col),
            out_shape=(
                jax.ShapeDtypeStruct((rows, cols, channels), jnp.bfloat16),
                jax.ShapeDtypeStruct((rows, BLOCK, channels), jnp.bfloat16),
                jax.ShapeDtypeStruct((rows, BLOCK, channels), jnp.float32),
            ),
            in_specs=[any_space] * 8,
            out_specs=[any_space] * 3,
            scratch_shapes=[
                pltpu.VMEM((chunks, own * n, BLOCK, channels), jnp.bfloat16),
                pltpu.VMEM((chunks, n, BLOCK, channels), jnp.bfloat16),
                pltpu.VMEM((chunks - 1, rows + 2, BLOCK, channels), jnp.bfloat16),
                block,
                block,
                pltpu.VMEM((chunks - 1, rows, BLOCK, channels), jnp.bfloat16),
                pltpu.VMEM((rows, BLOCK, channels), jnp.float32),
                square,
                square,
                square,
                square,
                pltpu.VMEM((3, channels, channels), jnp.bfloat16),
                pltpu.VMEM((1, channels), jnp.float32),
                pltpu.VMEM(w_depth.shape, jnp.float32),
                dma((7,)),
                dma((chunks,)),
                dma,
                dma((chunks,)),
                dma((chunks,)),
                dma,
                dma((chunks,)),
                dma((2,)),
                dma((2,)),
                dma((chunks,)),
                pltpu.SemaphoreType.REGULAR((half + 1,)),
                pltpu.SemaphoreType.REGULAR((half + 1,)),
            ],
            compiler_params=pltpu.CompilerParams(collective_id=0, has_side_effects=True),
        )(video, norm_gain.reshape(1, channels), w_query, w_key, w_value, w_out, w_time, w_depth)
        return pl.pallas_call(
            finish,
            out_shape=jax.ShapeDtypeStruct((1, rows, cols, channels), jnp.bfloat16),
            in_specs=[any_space] * 4,
            out_specs=any_space,
            scratch_shapes=[
                pltpu.VMEM((rows, cols, channels), jnp.bfloat16),
                block,
                pltpu.VMEM((rows, BLOCK, channels), jnp.float32),
                pltpu.VMEM(w_depth.shape, jnp.float32),
                dma((PIECES, 4)),
                dma((PIECES,)),
                dma,
            ],
        )(done, middle, edges, w_depth)

    return jax.shard_map(
        local,
        mesh=mesh,
        in_specs=(P("frm", None, "col", None), P(), P(), P(), P(), P(), P(), P()),
        out_specs=P("frm", None, "col", None),
        check_vma=False,
    )
```

```python
import functools
import math

import jax
import jax.numpy as jnp
from jax import lax
from jax.experimental import pallas as pl
from jax.experimental.pallas import tpu as pltpu
from jax.sharding import PartitionSpec as P

MESH = pl.DeviceIdType.MESH
EPSILON = 1e-06
BLOCK = 8
NEAR = 2
LANES = 256
PIECES = 2


def attend(slab, gain, w_query, w_key, w_value, w_out):
    rows, channels = slab.shape
    scale = lax.rsqrt(jnp.mean(slab * slab, axis=-1, keepdims=True) + EPSILON)
    normed = (slab * scale * gain).astype(jnp.bfloat16)
    queries = jnp.dot(normed, w_query, preferred_element_type=jnp.float32).astype(jnp.bfloat16)
    key_proj = jnp.dot(normed, w_key, preferred_element_type=jnp.float32).astype(jnp.bfloat16)
    values = jnp.dot(normed, w_value, preferred_element_type=jnp.float32).astype(jnp.bfloat16)
    scores = lax.dot_general(
        queries, key_proj, (((1,), (1,)), ((), ())), preferred_element_type=jnp.float32
    ) * (1.0 / math.sqrt(channels))
    ahead = lax.broadcasted_iota(jnp.int32, (rows, rows), 0) - lax.broadcasted_iota(
        jnp.int32, (rows, rows), 1
    )
    seen = (ahead >= 0) & ((ahead & (BLOCK - 1)) == 0)
    scores = jnp.where(seen, scores, -1e30)
    raised = jnp.exp(scores - jnp.max(scores, axis=-1, keepdims=True))
    weights = (raised / jnp.sum(raised, axis=-1, keepdims=True)).astype(jnp.bfloat16)
    attended = jnp.dot(weights, values, preferred_element_type=jnp.float32).astype(jnp.bfloat16)
    return slab + jnp.dot(attended, w_out, preferred_element_type=jnp.float32)


def time_conv(mixed, w_time):
    rows, channels = mixed.shape
    pairs = mixed.reshape(rows // (2 * BLOCK), 2 * BLOCK, channels)
    even = pairs[:, :BLOCK].reshape(rows // 2, channels)
    odd = pairs[:, BLOCK:].reshape(rows // 2, channels)
    prior = jnp.concatenate([even[:BLOCK], odd[:-BLOCK]], axis=0)
    summed = jnp.dot(prior.astype(jnp.bfloat16), w_time[0], preferred_element_type=jnp.float32)
    summed += jnp.dot(even.astype(jnp.bfloat16), w_time[1], preferred_element_type=jnp.float32)
    summed += jnp.dot(odd.astype(jnp.bfloat16), w_time[2], preferred_element_type=jnp.float32)
    return summed / (1.0 + jnp.exp(-summed))


def exchange(
    n,
    n_col,
    video,
    gain_in,
    w_query,
    w_key,
    w_value,
    w_out,
    w_time,
    w_depth_in,
    done,
    middle,
    edges,
    slabs,
    acts,
    frame,
    low_rim,
    high_rim,
    filtered,
    partial,
    wq,
    wk,
    wv,
    wo,
    wt,
    gain,
    w_depth,
    weight_sem,
    own_sem,
    slab_send,
    slab_recv,
    own_act_sem,
    act_send,
    act_recv,
    rim_send,
    rim_recv,
    done_sem,
    right_known,
    left_known,
):
    me = lax.axis_index("frm")
    col = lax.axis_index("col")
    chunks, frames, _, channels = slabs.shape
    chips = n // 2
    rows = n
    chip, core = me // 2, me % 2
    far = chips // 2

    weights = [
        pltpu.make_async_copy(source, target, weight_sem.at[i])
        for i, (source, target) in enumerate(
            (
                (w_query, wq),
                (w_key, wk),
                (w_value, wv),
                (w_out, wo),
                (w_time, wt),
                (gain_in, gain),
                (w_depth_in, w_depth),
            )
        )
    ]

    def device(away, other):
        return (chip + away + chips) % chips * 2 + (core + other) % 2

    barrier = pltpu.get_barrier_semaphore()
    for away in (1, -1):
        for other in (0, 1):
            pl.semaphore_signal(
                barrier, inc=1, device_id={"frm": device(away, other)}, device_id_type=MESH
            )
    pl.semaphore_signal(barrier, inc=1, device_id={"frm": device(0, 1)}, device_id_type=MESH)
    right, left = (col + 1) % n_col, (col + n_col - 1) % n_col
    for neighbour in (left, right):
        pl.semaphore_signal(barrier, inc=1, device_id={"col": neighbour}, device_id_type=MESH)

    def columns(step):
        return pl.ds(pl.multiple_of((step * (chunks - 1)) % chunks * BLOCK, BLOCK), BLOCK)

    def own_slab(step):
        return pltpu.make_async_copy(
            video.at[:, me, columns(step)], slabs.at[step, pl.ds(2 * me, 2)], own_sem.at[step]
        )

    for copy in weights:
        copy.start()
    for step in range(chunks):
        own_slab(step).start()

    pl.semaphore_wait(barrier, 7)

    def send_slab(step, to):
        pltpu.make_async_remote_copy(
            src_ref=video.at[:, to, columns(step)],
            dst_ref=slabs.at[step, pl.ds(2 * me, 2)],
            send_sem=slab_send,
            recv_sem=slab_recv.at[step],
            device_id={"frm": to},
            device_id_type=MESH,
        ).start()

    def send_slabs(first, last, away):
        @pl.loop(first, last)
        def _(step):
            for side in (1, -1) if away < far else (1,):
                for other in (0, 1):
                    send_slab(step, device(side * away, other))

    for away in range(1, far + 1):
        for side, known, reach in ((1, right_known, far), (-1, left_known, far - 1)):
            if 1 < away <= reach:
                pl.semaphore_wait(known.at[away], 1)
            if away < reach:
                pl.semaphore_signal(
                    known.at[away + 1],
                    inc=1,
                    device_id={"frm": device(-side, 0)},
                    device_id_type=MESH,
                )
        send_slabs(0, chunks if away <= NEAR else 1, away)
        if away == 1:

            @pl.loop(0, chunks)
            def _(step):
                send_slab(step, device(0, 1))

    @pl.loop(1, chunks)
    def _(step):
        @pl.loop(NEAR + 1, far)
        def _(away):
            for side in (1, -1):
                for other in (0, 1):
                    send_slab(step, device(side * away, other))

        for other in (0, 1):
            send_slab(step, device(far, other))

    for copy in weights:
        copy.wait()

    def partner(turn):
        hop, other = (turn + 1) // 2, (turn + 1) % 2
        return device((hop + 1) // 2 * (2 * (hop % 2) - 1), other)

    def landing(step, row):
        return middle.at[row] if step == chunks - 1 else frame.at[step, row + 1]

    def own_act(step):
        return pltpu.make_async_copy(acts.at[step, me], landing(step, me), own_act_sem.at[step])

    def send_acts(step, recv_step, target):
        @pl.loop(0, n - 1)
        def _(turn):
            to = partner(n - 2 - turn)
            pltpu.make_async_remote_copy(
                src_ref=acts.at[step, to],
                dst_ref=target,
                send_sem=act_send,
                recv_sem=act_recv.at[recv_step],
                device_id={"frm": to},
                device_id_type=MESH,
            ).start()

    for edge in (0, rows + 1):
        frame[:, edge] = jnp.zeros((chunks - 1, BLOCK, channels), frame.dtype)

    @pl.loop(0, chunks)
    def _(step):
        own_slab(step).wait()
        arrived = slabs.at[step, pl.ds(0, frames - 2)]
        pltpu.make_async_copy(arrived, arrived, slab_recv.at[step]).wait()
        slab = slabs[step].astype(jnp.float32).reshape(frames * BLOCK, channels)
        mixed = attend(slab, gain[...], wq[...], wk[...], wv[...], wo[...])
        activated = time_conv(mixed, wt)
        acts[step] = activated.reshape(rows, BLOCK, channels).astype(acts.dtype)

        @pl.when(step < chunks - 1)
        def _():
            pltpu.make_async_copy(
                acts.at[step, me], frame.at[step, me + 1], own_act_sem.at[step]
            ).start()
            send_acts(step, step, frame.at[step, me + 1])

        @pl.when(step == chunks - 1)
        def _():
            own_act(chunks - 1).start()
            send_acts(chunks - 1, chunks - 1, middle.at[me])

    def wait_frame(step):
        own_act(step).wait()
        ref = middle if step == chunks - 1 else frame.at[step]
        arrived = ref.at[pl.ds(0, rows - 1)]
        pltpu.make_async_copy(arrived, arrived, act_recv.at[step]).wait()

    def rim(step, target, neighbour):
        return pltpu.make_async_remote_copy(
            src_ref=frame.at[step],
            dst_ref=target,
            send_sem=rim_send.at[step],
            recv_sem=rim_recv.at[step],
            device_id={"col": neighbour},
            device_id_type=MESH,
        )

    to_left, to_right = rim(0, high_rim, left), rim(1, low_rim, right)
    wait_frame(0)
    to_left.start()
    wait_frame(1)
    to_right.start()
    wait_frame(2)
    to_left.wait()
    to_right.wait()

    has_left, has_right = col > 0, col < n_col - 1
    place = lax.broadcasted_iota(jnp.int32, (BLOCK, LANES), 0)

    @pl.loop(0, rows)
    def _(row):
        for lane in range(0, channels, LANES):
            span = pl.ds(lane, LANES)

            def column_sum(ref, b):
                total = None
                for a in range(3):
                    term = ref[row + a, :, span].astype(jnp.float32) * w_depth[a, pl.ds(b, 1), span]
                    total = term if total is None else total + term
                return total

            first, third, fourth = frame.at[0], frame.at[2], frame.at[1]
            first_0, first_1, first_2 = (column_sum(first, b) for b in range(3))
            third_0, third_1, third_2 = (column_sum(third, b) for b in range(3))
            fourth_0, fourth_1, fourth_2 = (column_sum(fourth, b) for b in range(3))
            low = pltpu.roll(column_sum(low_rim, 0), 1, 0)
            high = pltpu.roll(column_sum(high_rim, 2), BLOCK - 1, 0)
            low = jnp.where(has_left, low, 0.0)
            high = jnp.where(has_right, high, 0.0)

            def before(own, previous):
                return jnp.where(place == 0, previous, pltpu.roll(own, 1, 0))

            def after(own, following):
                return jnp.where(place == BLOCK - 1, following, pltpu.roll(own, BLOCK - 1, 0))

            first_part = before(first_0, low) + first_1
            third_part = third_1 + after(third_2, pltpu.roll(fourth_2, BLOCK - 1, 0))
            fourth_part = before(fourth_0, pltpu.roll(third_0, 1, 0)) + fourth_1
            filtered[0, row, :, span] = (first_part + pltpu.roll(first_2, BLOCK - 1, 0)).astype(
                filtered.dtype
            )
            filtered[2, row, :, span] = (third_part + pltpu.roll(third_0, 1, 0)).astype(
                filtered.dtype
            )
            filtered[1, row, :, span] = (fourth_part + after(fourth_2, high)).astype(filtered.dtype)
            kept = jnp.where(place == 0, third_part, first_part)
            kept = jnp.where(place == 1, pltpu.roll(first_0, 2, 0), kept)
            kept = jnp.where(place == BLOCK - 2, pltpu.roll(third_2, BLOCK - 2, 0), kept)
            partial[row, :, span] = kept

    stores = [
        pltpu.make_async_copy(
            filtered.at[step], done.at[:, columns(step)], done_sem.at[step]
        )
        for step in range(chunks - 1)
    ]
    stores.append(pltpu.make_async_copy(partial, edges, done_sem.at[chunks - 1]))
    for copy in stores:
        copy.start()
    for copy in stores:
        copy.wait()
    sent = slabs.at[:, pl.ds(0, frames - 2)]
    pltpu.make_async_copy(sent, sent, slab_send).wait()
    wait_frame(chunks - 1)
    sent = acts.at[:, pl.ds(0, rows - 1)]
    pltpu.make_async_copy(sent, sent, act_send).wait()


def finish(
    done, middle, edges, w_depth_in, out, image, inner, partial, w_depth, sems, out_sems, taps_sem
):
    rows, width, channels = done.shape
    band = rows // PIECES

    def load(piece, i):
        here = pl.ds(piece * band, band)
        if i == 0:
            source, target = middle.at[here], inner.at[pl.ds(piece * band + 1, band)]
        elif i == 1:
            source, target = edges.at[here], partial.at[here]
        else:
            span = pl.ds(0, BLOCK) if i == 2 else pl.ds(2 * BLOCK, 2 * BLOCK)
            source, target = done.at[here, span], image.at[here, span]
        return pltpu.make_async_copy(source, target, sems.at[piece, i])

    def store(piece):
        here = pl.ds(piece * band, band)
        return pltpu.make_async_copy(image.at[here], out.at[0, here], out_sems.at[piece])

    for piece in range(PIECES):
        for i in range(4):
            load(piece, i).start()
        if piece == 0:
            taps = pltpu.make_async_copy(w_depth_in, w_depth, taps_sem)
            taps.start()
    for edge in (0, rows + 1):
        inner[edge] = jnp.zeros(inner.shape[1:], inner.dtype)
    place = lax.broadcasted_iota(jnp.int32, (BLOCK, LANES), 0)

    taps.wait()
    for piece in range(PIECES):
        for i in range(1 if piece else 0, 4):
            load(piece, i).wait()
        if piece + 1 < PIECES:
            load(piece + 1, 0).wait()

        @pl.loop(piece * band, (piece + 1) * band)
        def _(row):
            for lane in range(0, channels, LANES):
                span = pl.ds(lane, LANES)
                lines = [inner[row + a, :, span].astype(jnp.float32) for a in range(3)]
                sums = []
                for b in range(3):
                    total = lines[0] * w_depth[0, pl.ds(b, 1), span]
                    for a in (1, 2):
                        total += lines[a] * w_depth[a, pl.ds(b, 1), span]
                    sums.append(total)
                kept = partial[row, :, span]
                before = pltpu.roll(sums[0], 1, 0)
                after = pltpu.roll(sums[2], BLOCK - 1, 0)
                total = sums[1] + jnp.where(place == 0, pltpu.roll(kept, BLOCK - 1, 0), before)
                total += jnp.where(place == BLOCK - 1, pltpu.roll(kept, 1, 0), after)
                first, third = pl.ds(0, BLOCK), pl.ds(2 * BLOCK, BLOCK)
                image[row, pl.ds(BLOCK, BLOCK), span] = total.astype(image.dtype)
                value = image[row, first, span].astype(jnp.float32)
                value = jnp.where(place == BLOCK - 1, kept + after, value)
                image[row, first, span] = value.astype(image.dtype)
                value = image[row, third, span].astype(jnp.float32)
                value = jnp.where(place == 0, kept + before, value)
                image[row, third, span] = value.astype(image.dtype)

        store(piece).start()
    for piece in range(PIECES):
        store(piece).wait()


def solution(mesh):
    n, n_col = mesh.shape["frm"], mesh.shape["col"]

    def local(video, norm_gain, w_query, w_key, w_value, w_out, w_time, w_depth):
        own, rows, cols, channels = video.shape
        chunks = cols // BLOCK
        half = n // 4
        any_space = pl.BlockSpec(memory_space=pl.ANY)
        square = pltpu.VMEM((channels, channels), jnp.bfloat16)
        dma = pltpu.SemaphoreType.DMA
        block = pltpu.VMEM((rows + 2, BLOCK, channels), jnp.bfloat16)
        done, middle, edges = pl.pallas_call(
            functools.partial(exchange, n, n_col),
            out_shape=(
                jax.ShapeDtypeStruct((rows, cols, channels), jnp.bfloat16),
                jax.ShapeDtypeStruct((rows, BLOCK, channels), jnp.bfloat16),
                jax.ShapeDtypeStruct((rows, BLOCK, channels), jnp.float32),
            ),
            in_specs=[any_space] * 8,
            out_specs=[any_space] * 3,
            scratch_shapes=[
                pltpu.VMEM((chunks, own * n, BLOCK, channels), jnp.bfloat16),
                pltpu.VMEM((chunks, n, BLOCK, channels), jnp.bfloat16),
                pltpu.VMEM((chunks - 1, rows + 2, BLOCK, channels), jnp.bfloat16),
                block,
                block,
                pltpu.VMEM((chunks - 1, rows, BLOCK, channels), jnp.bfloat16),
                pltpu.VMEM((rows, BLOCK, channels), jnp.float32),
                square,
                square,
                square,
                square,
                pltpu.VMEM((3, channels, channels), jnp.bfloat16),
                pltpu.VMEM((1, channels), jnp.float32),
                pltpu.VMEM(w_depth.shape, jnp.float32),
                dma((7,)),
                dma((chunks,)),
                dma,
                dma((chunks,)),
                dma((chunks,)),
                dma,
                dma((chunks,)),
                dma((2,)),
                dma((2,)),
                dma((chunks,)),
                pltpu.SemaphoreType.REGULAR((half + 1,)),
                pltpu.SemaphoreType.REGULAR((half + 1,)),
            ],
            compiler_params=pltpu.CompilerParams(collective_id=0, has_side_effects=True),
        )(video, norm_gain.reshape(1, channels), w_query, w_key, w_value, w_out, w_time, w_depth)
        return pl.pallas_call(
            finish,
            out_shape=jax.ShapeDtypeStruct((1, rows, cols, channels), jnp.bfloat16),
            in_specs=[any_space] * 4,
            out_specs=any_space,
            scratch_shapes=[
                pltpu.VMEM((rows, cols, channels), jnp.bfloat16),
                block,
                pltpu.VMEM((rows, BLOCK, channels), jnp.float32),
                pltpu.VMEM(w_depth.shape, jnp.float32),
                dma((PIECES, 4)),
                dma((PIECES,)),
                dma,
            ],
        )(done, middle, edges, w_depth)

    return jax.shard_map(
        local,
        mesh=mesh,
        in_specs=(P("frm", None, "col", None), P(), P(), P(), P(), P(), P(), P()),
        out_specs=P("frm", None, "col", None),
        check_vma=False,
    )
```
